32 devices in a mesh: line: 8 (over z, y), bus: 4 (over x, core).
Axes of the slice: x: 2, y: 2, z: 4, core: 2. Of those that a mesh axis runs over, the one named last changes fastest.
Arguments:
- clearness: float32 [192, 8192], P(None, ('line', 'bus')), may hold values from 0.05 to 0.8
- cos_zenith: float32 [192, 8192], P(None, ('line', 'bus')), may hold values from 0.05 to 1
- sun_azimuth: float32 [192, 8192], P(None, ('line', 'bus')), may hold values from -3.140625 to 3.140625
- dirint_cell: int32 [192, 8192], P(None, ('line', 'bus')), may hold values from 0 to 1259
- sky_bin: int32 [192, 8192], P(None, ('line', 'bus')), may hold values from 0 to 7
- dirint_coef: float32 [1260], replicated, may hold values from 0.5 to 1.5
- perez_coef: float32 [6, 8], replicated, may hold values from -0.3 to 0.6
- tilt_class: int32 [8192], P(('line', 'bus')), may hold values from 0 to 7
- azimuth_class: int32 [8192], P(('line', 'bus')), may hold values from 0 to 11
- tilt_table: float32 [8], replicated, may hold values from 0 to 1
- azimuth_table: float32 [12], replicated, may hold values from -3.140625 to 3.140625
- capacity: float32 [8192], P(('line', 'bus')), may hold values from 0.2 to 2
- site_bus: int32 [8192], P(('line', 'bus')), may hold values from 0 to 70143, as said below
- transfer_factors: bfloat16 [16000, 70144], P('line', 'bus'), may hold values from -0.0234375 to 0.0234375
Outputs:
- flows: float32 [16000, 192], P('line', 'bus')
The draws below stay inside these ranges and needn't reach their ends.
Inputs may be any that keep to these rules, and one draw needn't show every extreme that they name: `site_bus`: bus b lies in group b // 2192. In every aligned block of 256 sites at most 16 sites connect to buses of one group, and one group receives exactly 16 sites from every block.
All inputs are finite; a program needn't handle non-finite values.
Results may differ from the reference program's by a relative error of at most 0.0034.
Values may be sent and summed in bfloat16 or wider, within the bound.
No kernel may reach another device: no remote copies, remote signals or barrier semaphores. Data moves between devices by JAX's collectives and lax.ppermute only.
A program may use at most 128 MiB of HBM per device.

```python
import math
import jax
import jax.numpy as jnp
from jax import lax

LINES = 16000
BUSES = 70144
HOURS = 192
SITES_DEV = 256
DCELLS = 1260
SKYBINS = 8
TILTS = 8
AZIMS = 12
SITES = 8192
BUS_DEV = 2192
CAP = 16


def draw_site_bus(key, part):
    owners = SITES // SITES_DEV
    slots = owners * CAP
    keys = jax.random.split(jax.random.fold_in(key, 17), 5)
    forced = jax.random.randint(keys[0], (), 0, owners)
    popular = jax.random.randint(keys[1], (owners,), 0, 4)
    noise = jax.random.randint(keys[2], (owners, owners, CAP), 0, 2 ** 17)
    owner_ids = jnp.arange(owners, dtype=jnp.int32)
    score = noise + popular[None, :, None] * 2 ** 15 + (owner_ids == forced).astype(jnp.int32)[None, :, None] * 2 ** 18
    flat = score.reshape(owners, slots) * slots + jnp.arange(slots, dtype=jnp.int32)[None, :]
    order = jnp.argsort(-flat, axis=1)[:, :SITES_DEV]
    chosen = (order // CAP).astype(jnp.int32)
    local_bus = jax.random.randint(keys[3], (owners, SITES_DEV), 0, BUS_DEV)
    mixing = jax.random.randint(keys[4], (owners, SITES_DEV), 0, 2 ** 20) * SITES_DEV + jnp.arange(SITES_DEV, dtype=jnp.int32)[None, :]
    shuffle = jnp.argsort(mixing, axis=1)
    shuffled = jnp.take_along_axis(chosen, shuffle, axis=1)
    return (shuffled * BUS_DEV + local_bus).reshape(-1).astype(jnp.int32)


def set_ends(values, stream_key, low, top_value):
    shape = values.shape
    index_at = [jax.random.randint(jax.random.fold_in(stream_key, axis), (), 0, shape[axis]) for axis in range(len(shape))]
    values = values.at[tuple(index_at)].set(low)
    longest = shape.index(max(shape))
    index_at[longest] = (index_at[longest] + 1) % shape[longest]
    return values.at[tuple(index_at)].set(top_value)


def block_levels(rng, dims, shards, smallest, largest):
    def one(axis_at, parts):
        steps = jax.random.uniform(jax.random.fold_in(jax.random.fold_in(rng, 6), axis_at), (parts,), jnp.float32, smallest / len(shards), largest / len(shards))
        return jnp.repeat(jnp.exp(steps), dims[axis_at] // parts).reshape((-1,) + (1,) * (len(dims) - axis_at - 1))

    factor_of = one(*shards[0])
    for cut in shards[1:]:
        factor_of = factor_of * one(*cut)
    return factor_of


def bell_draw(key, shape, scale, most, pieces=(), kind=jnp.bfloat16):
    values = jax.random.normal(key, shape, jnp.float32) * scale
    if len(pieces) > 0:
        values = block_levels(key, shape, pieces, -0.22, 0.18) * values
    return jnp.clip(values, min=-most, max=most).astype(kind)


def setup_inputs(seed: int = 0) -> dict:
    streams_of = jax.random.split(jax.random.key(seed), 15)
    clearness = jnp.clip(0.05 + 0.75 * jax.random.uniform(streams_of[0], (HOURS, SITES), jnp.float32) ** block_levels(streams_of[0], (HOURS, SITES), ((1, 32),), -0.2, 0.2), 0.05, 0.8)
    cos_zenith = jnp.clip(0.05 + 0.95 * jax.random.uniform(streams_of[1], (HOURS, SITES), jnp.float32) ** block_levels(streams_of[1], (HOURS, SITES), ((1, 32),), -0.2, 0.2), 0.05, 1.0)
    sun_azimuth = jnp.clip(jax.random.uniform(streams_of[2], (HOURS, SITES), jnp.float32, -3.140625, 3.140625), -3.140625, 3.140625)
    dirint_cell = set_ends(jax.random.randint(streams_of[3], (HOURS, SITES), 0, DCELLS), jax.random.fold_in(streams_of[3], 1), 0, DCELLS - 1).astype(jnp.int32)
    sky_bin = set_ends(jax.random.randint(streams_of[4], (HOURS, SITES), 0, SKYBINS), jax.random.fold_in(streams_of[4], 1), 0, SKYBINS - 1).astype(jnp.int32)
    dirint_coef = jnp.clip(jnp.exp(jax.random.uniform(streams_of[5], (DCELLS,), jnp.float32, math.log(0.5), math.log(1.5))), 0.5, 1.5)
    perez_coef = jnp.clip(jax.random.uniform(streams_of[6], (6, SKYBINS), jnp.float32, -0.3, 0.6), -0.3, 0.6)
    tilt_class = set_ends(jax.random.randint(streams_of[7], (SITES,), 0, TILTS), jax.random.fold_in(streams_of[7], 1), 0, TILTS - 1).astype(jnp.int32)
    azimuth_class = set_ends(jax.random.randint(streams_of[8], (SITES,), 0, AZIMS), jax.random.fold_in(streams_of[8], 1), 0, AZIMS - 1).astype(jnp.int32)
    tilt_table = jnp.clip(jax.random.uniform(streams_of[9], (TILTS,), jnp.float32, 0.0, 1.0), 0.0, 1.0)
    azimuth_table = jnp.clip(jax.random.uniform(streams_of[10], (AZIMS,), jnp.float32, -3.140625, 3.140625), -3.140625, 3.140625)
    capacity = jnp.clip(jnp.exp(math.log(2.0) - 2.3025851 * jax.random.uniform(streams_of[11], (SITES,), jnp.float32) ** block_levels(streams_of[11], (SITES,), ((0, 32),), -0.2, 0.2)), 0.2, 2.0)
    site_bus = draw_site_bus(jax.random.fold_in(streams_of[14], 71), 0)
    transfer_factors = bell_draw(streams_of[13], (LINES, BUSES), BUSES ** -0.5, 0.0234375, ((0, 8), (1, 4)))
    return dict(clearness=clearness, cos_zenith=cos_zenith, sun_azimuth=sun_azimuth, dirint_cell=dirint_cell, sky_bin=sky_bin, dirint_coef=dirint_coef, perez_coef=perez_coef, tilt_class=tilt_class, azimuth_class=azimuth_class, tilt_table=tilt_table, azimuth_table=azimuth_table, capacity=capacity, site_bus=site_bus, transfer_factors=transfer_factors)


solar_constant = 1367.0
albedo = 0.2
cos_limit = 0.08716


def pick_table(classes, table, count):
    picked = jnp.zeros(classes.shape, jnp.float32)
    for entry in range(count):
        picked = jnp.where(classes == entry, table[entry], picked)
    return picked


def site_power(clear, cosz, sun_az, cell, sky, tilt_angle, array_azimuth, site_capacity, dirint_coef, perez_coef):
    global_flat = clear * solar_constant * cosz
    zenith = jnp.arccos(cosz)
    airmass = 1.0 / (cosz + 0.50572 * (96.07995 - zenith * (180.0 / math.pi)) ** -1.6364)
    clear_beam = 0.866 - 0.122 * airmass + 0.0121 * airmass ** 2 - 0.000653 * airmass ** 3 + 0.000014 * airmass ** 4
    part_a = 0.512 - 1.56 * clear + 2.286 * clear ** 2 - 2.222 * clear ** 3
    part_b = 0.37 + 0.962 * clear
    part_c = -0.28 + 0.932 * clear - 2.048 * clear ** 2
    beam_index = jnp.maximum(clear_beam - (part_a + part_b * jnp.exp(part_c * airmass)), 0.0)
    direct_normal = solar_constant * beam_index * jnp.take(dirint_coef, cell)
    diffuse = jnp.maximum(global_flat - direct_normal * cosz, 0.1 * global_flat)
    brightness = diffuse * airmass / solar_constant
    factors = [jnp.zeros(cosz.shape, jnp.float32) for entry in range(6)]
    for bin_index in range(perez_coef.shape[1]):
        hit = sky == bin_index
        factors = [jnp.where(hit, perez_coef[row, bin_index], factors[row]) for row in range(6)]
    circumsolar = jnp.maximum(0.0, factors[0] + factors[1] * brightness + factors[2] * zenith)
    horizon_term = factors[3] + factors[4] * brightness + factors[5] * zenith
    cos_tilt = jnp.cos(tilt_angle)
    sin_tilt = jnp.sin(tilt_angle)
    cos_incidence = cosz * cos_tilt + jnp.sin(zenith) * sin_tilt * jnp.cos(sun_az - array_azimuth)
    facing = jnp.maximum(cos_incidence, 0.0)
    horizon_cos = jnp.maximum(cosz, cos_limit)
    sky_part = diffuse * ((1.0 - circumsolar) * (1.0 + cos_tilt) * 0.5 + circumsolar * facing / horizon_cos + horizon_term * sin_tilt)
    plane = direct_normal * facing + sky_part + albedo * global_flat * (1.0 - cos_tilt) * 0.5
    return (site_capacity * plane / 1000.0).astype(jnp.bfloat16)


def reference(clearness, cos_zenith, sun_azimuth, dirint_cell, sky_bin, dirint_coef, perez_coef, tilt_class, azimuth_class, tilt_table, azimuth_table, capacity, site_bus, transfer_factors):
    tilt_angle = pick_table(tilt_class, tilt_table, TILTS)
    array_azimuth = pick_table(azimuth_class, azimuth_table, AZIMS)

    def one_hour(hour_row):
        clear, cosz, sun_az, cell, sky = hour_row
        power = site_power(clear, cosz, sun_az, cell, sky, tilt_angle, array_azimuth, capacity, dirint_coef, perez_coef)
        return jax.ops.segment_sum(power.astype(jnp.float32), site_bus, num_segments=BUSES)

    summed = lax.map(one_hour, (clearness, cos_zenith, sun_azimuth, dirint_cell, sky_bin))
    injection = summed.astype(jnp.bfloat16)
    return jnp.dot(transfer_factors, injection.T, preferred_element_type=jnp.float32)
```

```python
import functools
import math

import jax
import jax.numpy as jnp
from jax import lax
from jax.experimental import pallas as pl
from jax.experimental.pallas import tpu as pltpu
from jax.sharding import PartitionSpec as P

BUSES = 70144
TILTS = 8
AZIMS = 12


solar_constant = 1367.0
albedo = 0.2
cos_limit = 0.08716
row_width = 36


def pick_table(classes, table, count):
    picked = jnp.zeros(classes.shape, jnp.float32)
    for entry in range(count):
        picked = jnp.where(classes == entry, table[entry], picked)
    return picked


def dirint_lookup(cell, dirint_coef):
    row_count = dirint_coef.shape[0] // row_width
    table = dirint_coef.reshape(row_count, row_width)
    flat_cell = cell.reshape(-1)
    upper = flat_cell // row_width
    lower = flat_cell % row_width
    row_pick = (upper[:, None] == jnp.arange(row_count, dtype=jnp.int32)[None, :]).astype(
        jnp.float32
    )
    rows = jnp.dot(
        row_pick, table, precision=lax.Precision.HIGHEST, preferred_element_type=jnp.float32
    )
    column_hit = lower[:, None] == jnp.arange(row_width, dtype=jnp.int32)[None, :]
    picked = jnp.sum(jnp.where(column_hit, rows, 0.0), axis=1)
    return picked.reshape(cell.shape)


def site_power(
    clear,
    cosz,
    sun_az,
    cell,
    sky,
    tilt_angle,
    array_azimuth,
    site_capacity,
    dirint_coef,
    perez_coef,
):
    global_flat = clear * solar_constant * cosz
    zenith = jnp.arccos(cosz)
    airmass = 1.0 / (cosz + 0.50572 * (96.07995 - zenith * (180.0 / math.pi)) ** (-1.6364))
    clear_beam = (
        0.866 - 0.122 * airmass + 0.0121 * airmass**2 - 0.000653 * airmass**3 + 1.4e-05 * airmass**4
    )
    part_a = 0.512 - 1.56 * clear + 2.286 * clear**2 - 2.222 * clear**3
    part_b = 0.37 + 0.962 * clear
    part_c = -0.28 + 0.932 * clear - 2.048 * clear**2
    beam_index = jnp.maximum(clear_beam - (part_a + part_b * jnp.exp(part_c * airmass)), 0.0)
    direct_normal = solar_constant * beam_index * dirint_lookup(cell, dirint_coef)
    diffuse = jnp.maximum(global_flat - direct_normal * cosz, 0.1 * global_flat)
    brightness = diffuse * airmass / solar_constant
    factors = [jnp.zeros(cosz.shape, jnp.float32) for entry in range(6)]
    for bin_index in range(perez_coef.shape[1]):
        hit = sky == bin_index
        factors = [jnp.where(hit, perez_coef[row, bin_index], factors[row]) for row in range(6)]
    circumsolar = jnp.maximum(0.0, factors[0] + factors[1] * brightness + factors[2] * zenith)
    horizon_term = factors[3] + factors[4] * brightness + factors[5] * zenith
    cos_tilt = jnp.cos(tilt_angle)
    sin_tilt = jnp.sin(tilt_angle)
    cos_incidence = cosz * cos_tilt + jnp.sin(zenith) * sin_tilt * jnp.cos(sun_az - array_azimuth)
    facing = jnp.maximum(cos_incidence, 0.0)
    horizon_cos = jnp.maximum(cosz, cos_limit)
    sky_part = diffuse * (
        (1.0 - circumsolar) * (1.0 + cos_tilt) * 0.5
        + circumsolar * facing / horizon_cos
        + horizon_term * sin_tilt
    )
    plane = direct_normal * facing + sky_part + albedo * global_flat * (1.0 - cos_tilt) * 0.5
    return (site_capacity * plane / 1000.0).astype(jnp.bfloat16)


def general_device(
    clearness,
    cos_zenith,
    sun_azimuth,
    dirint_cell,
    sky_bin,
    dirint_coef,
    perez_coef,
    tilt_class,
    azimuth_class,
    tilt_table,
    azimuth_table,
    capacity,
    site_bus,
    transfer_factors,
):
    line_count = lax.axis_size("line")
    bus_count = lax.axis_size("bus")
    owners = line_count * bus_count
    n_hours, n_sites = clearness.shape
    group_buses = BUSES // owners
    slots_each = max(2, 2 * n_sites // owners)
    tilt_angle = pick_table(tilt_class, tilt_table, TILTS)
    array_azimuth = pick_table(azimuth_class, azimuth_table, AZIMS)
    power = site_power(
        clearness,
        cos_zenith,
        sun_azimuth,
        dirint_cell,
        sky_bin,
        tilt_angle,
        array_azimuth,
        capacity,
        dirint_coef,
        perez_coef,
    )
    group_index = site_bus // group_buses
    target = group_index % line_count * bus_count + group_index // line_count
    local_bus = site_bus % group_buses
    one_hot = (target[:, None] == jnp.arange(owners, dtype=jnp.int32)[None, :]).astype(jnp.int32)
    position = jnp.sum(one_hot * (jnp.cumsum(one_hot, axis=0) - 1), axis=1)
    slot_index = target * slots_each + position
    outgoing = jnp.zeros((n_hours, owners * slots_each), jnp.bfloat16).at[:, slot_index].set(power)
    labels = jnp.zeros((1, owners * slots_each), jnp.int32).at[0, slot_index].set(local_bus)
    arrived, bus_tags = (
        lax.all_to_all(outgoing, ("line", "bus"), split_axis=1, concat_axis=1, tiled=True),
        lax.all_to_all(labels, ("line", "bus"), split_axis=1, concat_axis=1, tiled=True),
    )
    bus_tags = bus_tags.reshape(owners * slots_each)
    member = (bus_tags[:, None] == jnp.arange(group_buses, dtype=jnp.int32)[None, :]).astype(
        jnp.bfloat16
    )
    injection = jnp.einsum("hr,rb->bh", arrived, member, preferred_element_type=jnp.float32).astype(
        jnp.bfloat16
    )
    partial_flows = jnp.dot(
        transfer_factors,
        lax.all_gather(injection, "line", axis=0, tiled=True),
        preferred_element_type=jnp.float32,
    )
    return lax.psum_scatter(partial_flows, "bus", scatter_dimension=1, tiled=True)


LANES = 128
ACOS_POLY = (
    1.5707963262615365,
    -0.21460172591625612,
    0.08904479608150453,
    -0.0507408012983321,
    0.033314914408815,
    -0.02284457168134235,
    0.014575916928409219,
    -0.00744564558483129,
    0.002518626106102872,
    -0.00040427332732297214,
)
COS_POLY = tuple((-1.0) ** k / math.factorial(2 * k) for k in range(8))
SIN_POLY = tuple((-1.0) ** k / math.factorial(2 * k + 1) for k in range(8))
EMPTY = 4095


def horner(x, poly):
    total = jnp.full_like(x, poly[-1])
    for coefficient in poly[-2::-1]:
        total = total * x + coefficient
    return total


def reduce_pi(x):
    turns = jnp.floor(x * (1.0 / math.pi) + 0.5)
    rest = (x - turns * 3.140625) - turns * 0.0009676535897932
    odd = turns - 2.0 * jnp.floor(turns * 0.5)
    return rest, 1.0 - 2.0 * odd


def cosine(x):
    rest, sign = reduce_pi(x)
    return sign * horner(rest * rest, COS_POLY)


def sine(x):
    rest, sign = reduce_pi(x)
    return sign * rest * horner(rest * rest, SIN_POLY)


def to_column(row, eye):
    return jnp.sum(jnp.where(eye, row, 0.0), axis=1, keepdims=True)


def place_kernel(bus_ref, slot_ref, tags_ref, *, owners, group_buses, cap, n_line, n_bus):
    n_sites = bus_ref.shape[1]
    bus = bus_ref[...]
    group = jnp.zeros(bus.shape, jnp.int32)
    for k in range(1, owners):
        group = group + (bus >= k * group_buses).astype(jnp.int32)
    local = (bus - group * group_buses).astype(jnp.float32)
    group = group.astype(jnp.float32)
    first = lax.broadcasted_iota(jnp.int32, (n_sites, n_sites), 0)
    second = lax.broadcasted_iota(jnp.int32, (n_sites, n_sites), 1)
    eye = first == second
    earlier = (to_column(group, eye) == group) & (first < second)
    position = jnp.sum(jnp.where(earlier, 1.0, 0.0), axis=0, keepdims=True)
    slot = group * float(cap) + position
    slot_ref[...] = slot.astype(jnp.int32)
    slot_column = to_column(slot, eye).astype(jnp.int32)
    local_column = to_column(local, eye)
    n_slots = n_line * cap
    for bus_index in range(n_bus):
        lanes = lax.broadcasted_iota(jnp.int32, (n_sites, n_slots), 1) + bus_index * n_slots
        hit = slot_column == lanes
        tag = jnp.sum(jnp.where(hit, local_column + 1.0, 0.0), axis=0, keepdims=True)
        tag = jnp.where(tag > 0.5, tag - 1.0, float(EMPTY)).astype(jnp.int32)
        for line_index in range(n_line):
            row = line_index * n_bus + bus_index
            tags_ref[row : row + 1, :] = tag


def place_sites(site_bus, owners, group_buses, cap, n_line, n_bus):
    n_sites = site_bus.shape[0]
    return pl.pallas_call(
        functools.partial(
            place_kernel,
            owners=owners,
            group_buses=group_buses,
            cap=cap,
            n_line=n_line,
            n_bus=n_bus,
        ),
        out_shape=(
            jax.ShapeDtypeStruct((1, n_sites), jnp.int32),
            jax.ShapeDtypeStruct((owners, n_line * cap), jnp.int32),
        ),
        cost_estimate=pl.CostEstimate(flops=10**6, bytes_accessed=10**5, transcendentals=0),
        name="place",
    )(site_bus.reshape(1, n_sites))


def power_kernel(
    tilt_ref,
    azimuth_ref,
    clear_ref,
    cosz_ref,
    sun_ref,
    cell_ref,
    sky_ref,
    dirint_ref,
    perez_ref,
    tilt_class_ref,
    azimuth_class_ref,
    capacity_ref,
    slot_ref,
    out_ref,
    power_ref,
    *,
    n_line,
    n_bus,
    cap,
    rows,
):
    n_hours, n_sites = clear_ref.shape
    tilt_class = tilt_class_ref[...]
    azimuth_class = azimuth_class_ref[...]
    tilt = jnp.zeros(tilt_class.shape, jnp.float32)
    for entry in range(TILTS):
        tilt = jnp.where(tilt_class == entry, tilt_ref[entry], tilt)
    azimuth = jnp.zeros(tilt_class.shape, jnp.float32)
    for entry in range(AZIMS):
        azimuth = jnp.where(azimuth_class == entry, azimuth_ref[entry], azimuth)
    wide = (rows, LANES)
    for part in range(n_sites // LANES):
        lanes = slice(part * LANES, (part + 1) * LANES)
        tilt_part = tilt[:, lanes]
        cos_tilt = jnp.broadcast_to(cosine(tilt_part), wide)
        sin_tilt = jnp.broadcast_to(sine(tilt_part), wide)
        array_azimuth = jnp.broadcast_to(azimuth[:, lanes], wide)
        site_capacity = jnp.broadcast_to(capacity_ref[:, lanes], wide)

        def step(index, carry):
            at = pl.ds(pl.multiple_of(index * rows, rows), rows)
            clear = clear_ref[at, lanes]
            cosz = cosz_ref[at, lanes]
            sun_az = sun_ref[at, lanes]
            cell = cell_ref[at, lanes]
            sky = sky_ref[at, lanes]
            global_flat = clear * solar_constant * cosz
            zenith = jnp.sqrt(1.0 - cosz) * horner(cosz, ACOS_POLY)
            sin_zenith = jnp.sqrt((1.0 - cosz) * (1.0 + cosz))
            height = 96.07995 - zenith * (180.0 / math.pi)
            airmass = 1.0 / (cosz + 0.50572 * jnp.exp(-1.6364 * jnp.log(height)))
            clear_beam = horner(airmass, (0.866, -0.122, 0.0121, -0.000653, 1.4e-05))
            part_a = horner(clear, (0.512, -1.56, 2.286, -2.222))
            part_b = 0.37 + 0.962 * clear
            part_c = horner(clear, (-0.28, 0.932, -2.048))
            beam = jnp.maximum(clear_beam - (part_a + part_b * jnp.exp(part_c * airmass)), 0.0)
            low = cell & (LANES - 1)
            high = cell >> 7
            coefficient = jnp.zeros(wide, jnp.float32)
            for row in range(dirint_ref.shape[0]):
                line = jnp.broadcast_to(dirint_ref[row : row + 1, :], wide)
                found = jnp.take_along_axis(line, low, axis=1, mode="promise_in_bounds")
                coefficient = jnp.where(high == row, found, coefficient)
            direct = solar_constant * beam * coefficient
            diffuse = jnp.maximum(global_flat - direct * cosz, 0.1 * global_flat)
            bright = diffuse * airmass * (1.0 / solar_constant)
            factor = [
                jnp.take_along_axis(
                    jnp.broadcast_to(perez_ref[row : row + 1, :], wide),
                    sky,
                    axis=1,
                    mode="promise_in_bounds",
                )
                for row in range(6)
            ]
            circumsolar = jnp.maximum(0.0, factor[0] + factor[1] * bright + factor[2] * zenith)
            horizon = factor[3] + factor[4] * bright + factor[5] * zenith
            facing = jnp.maximum(
                cosz * cos_tilt + sin_zenith * sin_tilt * cosine(sun_az - array_azimuth), 0.0
            )
            sky_part = diffuse * (
                (1.0 - circumsolar) * (1.0 + cos_tilt) * 0.5
                + circumsolar * facing / jnp.maximum(cosz, cos_limit)
                + horizon * sin_tilt
            )
            plane = direct * facing + sky_part + albedo * global_flat * (1.0 - cos_tilt) * 0.5
            power_ref[at, lanes] = (site_capacity * plane / 1000.0).astype(jnp.bfloat16)
            return carry

        lax.fori_loop(0, n_hours // rows, step, 0)

    power = power_ref[...]
    low_hours = power[:LANES]
    rest = power[LANES:]
    blank = jnp.zeros_like(rest)
    left = jnp.concatenate([rest, blank], axis=0)
    right = jnp.concatenate([blank, rest], axis=0)
    slot = slot_ref[...]
    n_slots = n_line * cap
    half = cap // 2
    dims = (((1,), (1,)), ((), ()))
    for bus_index in range(n_bus):
        base = bus_index * n_slots
        slots = lax.broadcasted_iota(jnp.int32, (n_slots, n_sites), 0) + base
        pick = jnp.where(slots == slot, 1.0, 0.0).astype(jnp.bfloat16)
        top = lax.dot_general(pick, low_hours, dims, preferred_element_type=jnp.float32)
        index = lax.broadcasted_iota(jnp.int32, (n_slots // 2, n_sites), 0)
        paired = (index // half) * cap + index % half + base
        pick_left = jnp.where(paired == slot, 1.0, 0.0).astype(jnp.bfloat16)
        pick_right = jnp.where(paired + half == slot, 1.0, 0.0).astype(jnp.bfloat16)
        bottom = lax.dot_general(
            pick_left, left, dims, preferred_element_type=jnp.float32
        ) + lax.dot_general(pick_right, right, dims, preferred_element_type=jnp.float32)
        top = top.astype(jnp.bfloat16)
        bottom = bottom.astype(jnp.bfloat16)
        for line_index in range(n_line):
            row = line_index * n_bus + bus_index
            out_ref[row, :n_slots, :] = top
            out_ref[row, n_slots:, :] = bottom


def packed_power(
    tilt_table,
    azimuth_table,
    hourly,
    dirint_coef,
    perez_coef,
    tilt_class,
    azimuth_class,
    capacity,
    slot,
    n_line,
    n_bus,
    cap,
):
    n_hours, n_sites = hourly[0].shape
    owners = n_line * n_bus
    n_slots = n_line * cap
    rows_of = -(-dirint_coef.shape[0] // LANES)
    dirint = jnp.pad(dirint_coef, (0, rows_of * LANES - dirint_coef.shape[0]))
    dirint = dirint.reshape(rows_of, LANES)
    perez = jnp.pad(perez_coef, ((0, 2), (0, LANES - perez_coef.shape[1])))
    smem = pl.BlockSpec(memory_space=pltpu.SMEM)
    vmem = pl.BlockSpec(memory_space=pltpu.VMEM)
    return pl.pallas_call(
        functools.partial(power_kernel, n_line=n_line, n_bus=n_bus, cap=cap, rows=32),
        out_shape=jax.ShapeDtypeStruct((owners, n_slots * n_hours // LANES, LANES), jnp.bfloat16),
        in_specs=[smem, smem] + [vmem] * 11,
        out_specs=vmem,
        scratch_shapes=[pltpu.VMEM((n_hours, n_sites), jnp.bfloat16)],
        compiler_params=pltpu.CompilerParams(vmem_limit_bytes=32 << 20),
        cost_estimate=pl.CostEstimate(
            flops=2 * 10**8, bytes_accessed=3 * 10**6, transcendentals=2 * 10**5
        ),
        name="power",
    )(
        tilt_table,
        azimuth_table,
        *hourly,
        dirint,
        perez,
        tilt_class.reshape(1, n_sites),
        azimuth_class.reshape(1, n_sites),
        capacity.reshape(1, n_sites),
        slot,
    )


def order_kernel(tags_ref, sorted_ref, rank_ref):
    n_groups, n_slots = tags_ref.shape
    tags = tags_ref[...].astype(jnp.float32)
    columns = jnp.transpose(tags)
    lanes = lax.broadcasted_iota(jnp.int32, (n_slots, n_slots), 1)
    row_index = lax.broadcasted_iota(jnp.int32, (1, n_slots), 1).astype(jnp.float32)
    column_index = lax.broadcasted_iota(jnp.int32, (n_slots, 1), 0).astype(jnp.float32)
    for g in range(n_groups):
        column = columns[:, g : g + 1]
        key_row = tags[g : g + 1] * n_slots + row_index
        key_column = column * n_slots + column_index
        rank_row = jnp.sum(jnp.where(key_column < key_row, 1.0, 0.0), axis=0, keepdims=True)
        rank_column = jnp.sum(jnp.where(key_row < key_column, 1.0, 0.0), axis=1, keepdims=True)
        hit = rank_column.astype(jnp.int32) == lanes
        ordered = jnp.sum(jnp.where(hit, column, 0.0), axis=0, keepdims=True)
        sorted_ref[g : g + 1, :] = ordered.astype(jnp.int32)
        rank_ref[g : g + 1, :] = rank_row.astype(jnp.int32)


def order_slots(tags):
    shape = jax.ShapeDtypeStruct(tags.shape, jnp.int32)
    return pl.pallas_call(
        order_kernel,
        out_shape=(shape, shape),
        compiler_params=pltpu.CompilerParams(vmem_limit_bytes=32 << 20),
        cost_estimate=pl.CostEstimate(flops=10**7, bytes_accessed=10**5, transcendentals=0),
        name="order",
    )(tags)


def select_kernel(
    plan_ref, sorted_ref, factors_ref, out_ref, buffer, pick, sems, *, group_buses, window, seg
):
    g = pl.program_id(0)
    n_groups = pl.num_programs(0)
    n_slots = out_ref.shape[1]
    half = n_slots // 2
    n_seg = window // seg

    def copy(index):
        start = pl.multiple_of((index * group_buses) // LANES * LANES, LANES)
        slot = lax.rem(index, 2)
        return pltpu.make_async_copy(
            factors_ref.at[:, pl.ds(start, window)], buffer.at[slot], sems.at[slot]
        )

    @pl.when(g == 0)
    def _():
        copy(g).start()

    @pl.when(g + 1 < n_groups)
    def _():
        copy(g + 1).start()

    offset = lax.rem(g * group_buses, LANES)
    last_first = plan_ref[0, g]
    first_second = plan_ref[1, g]
    place = sorted_ref[pl.ds(g, 1), :] + offset

    def wanted(chunk, k):
        if chunk == 0:
            return k <= last_first
        return k >= first_second

    for chunk in range(2):
        columns = slice(chunk * half, (chunk + 1) * half)
        for k in range(n_seg):

            @pl.when(wanted(chunk, k))
            def _():
                buses = lax.broadcasted_iota(jnp.int32, (seg, half), 0) + k * seg
                pick[k * seg : (k + 1) * seg, columns] = jnp.where(
                    buses == place[:, columns], 1.0, 0.0
                ).astype(jnp.bfloat16)

    copy(g).wait()
    now = lax.rem(g, 2)
    for chunk in range(2):
        columns = slice(chunk * half, (chunk + 1) * half)
        for k in range(n_seg):

            @pl.when(wanted(chunk, k))
            def _():
                found = jnp.dot(
                    buffer[now, :, k * seg : (k + 1) * seg],
                    pick[k * seg : (k + 1) * seg, columns],
                    preferred_element_type=jnp.float32,
                ).astype(jnp.bfloat16)
                if chunk == 0:
                    begins = k == 0
                else:
                    begins = k == first_second

                @pl.when(begins)
                def _():
                    out_ref[:, columns] = found

                @pl.when(jnp.logical_not(begins))
                def _():
                    out_ref[:, columns] += found

    @pl.when(first_second >= n_seg)
    def _():
        out_ref[:, half:] = jnp.zeros((out_ref.shape[0], half), jnp.bfloat16)


def select_columns(plan, ordered, factors, group_buses, window, seg):
    n_groups, n_slots = ordered.shape
    n_lines = factors.shape[0]
    return pl.pallas_call(
        functools.partial(select_kernel, group_buses=group_buses, window=window, seg=seg),
        grid=(n_groups,),
        in_specs=[
            pl.BlockSpec(memory_space=pltpu.SMEM),
            pl.BlockSpec((n_groups, n_slots), lambda g: (0, 0)),
            pl.BlockSpec(memory_space=pl.ANY),
        ],
        out_specs=pl.BlockSpec((n_lines, n_slots), lambda g: (0, g)),
        out_shape=jax.ShapeDtypeStruct((n_lines, n_groups * n_slots), jnp.bfloat16),
        scratch_shapes=[
            pltpu.VMEM((2, n_lines, window), jnp.bfloat16),
            pltpu.VMEM((window, n_slots), jnp.bfloat16),
            pltpu.SemaphoreType.DMA((2,)),
        ],
        compiler_params=pltpu.CompilerParams(vmem_limit_bytes=48 << 20),
        cost_estimate=pl.CostEstimate(
            flops=2 * n_lines * window * n_groups * n_slots,
            bytes_accessed=2 * n_lines * window * n_groups,
            transcendentals=0,
        ),
        name="select",
    )(plan, ordered, factors)


def combine_kernel(plan_ref, core_ref, rank_ref, top_ref, bottom_ref, picked_ref, keep_ref, send_ref, acc, *, n_seg, n_bus):
    g = pl.program_id(0)
    n_lines, n_slots = picked_ref.shape
    half = n_slots // 2
    top = top_ref[...].reshape(n_slots, LANES)
    bottom = bottom_ref[...].astype(jnp.float32)
    blocks, rows, _ = bottom.shape
    turned = pltpu.roll(bottom.reshape(blocks * rows, LANES), LANES // 2, 1)
    bottom = jnp.concatenate([bottom, turned.reshape(blocks, rows, LANES)], axis=1)
    bottom = bottom.reshape(n_slots, LANES).astype(jnp.bfloat16)
    power = jnp.concatenate([top, bottom], axis=1)
    rank = rank_ref[pl.ds(g, 1), :]
    places = lax.broadcasted_iota(jnp.int32, (n_slots, n_slots), 0)
    move = jnp.where(places == rank, 1.0, 0.0).astype(jnp.bfloat16)
    power = jnp.dot(move, power, preferred_element_type=jnp.float32).astype(jnp.bfloat16)
    flow = jnp.dot(picked_ref[:, :half], power[:half], preferred_element_type=jnp.float32)

    @pl.when(g == 0)
    def _():
        acc[...] = jnp.zeros_like(acc)

    acc[:n_lines, :] += flow

    @pl.when(plan_ref[1, g] < n_seg)
    def _():
        acc[:n_lines, :] += jnp.dot(
            picked_ref[:, half:], power[half:], preferred_element_type=jnp.float32
        )

    @pl.when(g == pl.num_programs(0) - 1)
    def _():
        turned = jnp.transpose(acc[...])
        rows_each = keep_ref.shape[1]
        for x in range(n_bus // 2):
            pieces = [
                turned[(2 * x + c) * rows_each : (2 * x + c + 1) * rows_each] for c in range(2)
            ]

            @pl.when(core_ref[0] == 0)
            def _():
                keep_ref[x] = pieces[0]
                send_ref[x] = pieces[1]

            @pl.when(core_ref[0] == 1)
            def _():
                keep_ref[x] = pieces[1]
                send_ref[x] = pieces[0]


def combine(plan, core, rank, arrived, picked, n_bus, n_hours, n_seg, cap):
    n_groups, n_slots = rank.shape
    n_lines = picked.shape[0]
    owners = arrived.shape[0]
    padded = -(-n_lines // LANES) * LANES
    part = jax.ShapeDtypeStruct((n_bus // 2, n_hours // n_bus, padded), jnp.float32)
    smem = pl.BlockSpec(memory_space=pltpu.SMEM)
    offset = n_groups * cap // (cap // 2)
    whole = pl.BlockSpec(part.shape, lambda g: (0, 0, 0))
    return pl.pallas_call(
        functools.partial(combine_kernel, n_seg=n_seg, n_bus=n_bus),
        grid=(n_groups,),
        in_specs=[
            smem,
            smem,
            pl.BlockSpec((n_groups, n_slots), lambda g: (0, 0)),
            pl.BlockSpec((owners, cap, LANES), lambda g: (0, g, 0)),
            pl.BlockSpec((owners, cap // 2, LANES), lambda g: (0, offset + g, 0)),
            pl.BlockSpec((n_lines, n_slots), lambda g: (0, g)),
        ],
        out_specs=(whole, whole),
        out_shape=(part, part),
        scratch_shapes=[pltpu.VMEM((padded, 2 * LANES), jnp.float32)],
        compiler_params=pltpu.CompilerParams(vmem_limit_bytes=48 << 20),
        cost_estimate=pl.CostEstimate(
            flops=2 * n_lines * n_groups * n_slots * 256,
            bytes_accessed=2 * n_lines * n_groups * n_slots,
            transcendentals=0,
        ),
        name="combine",
    )(plan, core, rank, arrived, arrived, picked)


def finish_kernel(own_ref, other_ref, out_ref):
    total = own_ref[...] + other_ref[...].astype(jnp.float32)
    rows = out_ref.shape[1]
    blank = jnp.zeros((LANES - rows, total.shape[1]), jnp.float32)
    turned = jnp.transpose(jnp.concatenate([total, blank], axis=0))
    out_ref[...] = turned[: out_ref.shape[0], :rows]


def finish(own, other, n_lines):
    return pl.pallas_call(
        finish_kernel,
        out_shape=jax.ShapeDtypeStruct((n_lines, own.shape[0]), jnp.float32),
        compiler_params=pltpu.CompilerParams(vmem_limit_bytes=32 << 20),
        name="finish",
    )(own, other)


def fast_device(
    clearness,
    cos_zenith,
    sun_azimuth,
    dirint_cell,
    sky_bin,
    dirint_coef,
    perez_coef,
    tilt_class,
    azimuth_class,
    tilt_table,
    azimuth_table,
    capacity,
    site_bus,
    transfer_factors,
):
    n_line = lax.axis_size("line")
    n_bus = lax.axis_size("bus")
    owners = n_line * n_bus
    n_hours, n_sites = clearness.shape
    n_lines, n_columns = transfer_factors.shape
    group_buses = BUSES // owners
    cap = 2 * n_sites // owners
    window = window_of(group_buses)
    seg = window // 3
    slot, tags = place_sites(site_bus, owners, group_buses, cap, n_line, n_bus)
    tags = lax.all_to_all(tags, ("line", "bus"), split_axis=0, concat_axis=0, tiled=True)
    outgoing = packed_power(
        tilt_table,
        azimuth_table,
        (clearness, cos_zenith, sun_azimuth, dirint_cell, sky_bin),
        dirint_coef,
        perez_coef,
        tilt_class,
        azimuth_class,
        capacity,
        slot,
        n_line,
        n_bus,
        cap,
    )
    arrived = lax.all_to_all(outgoing, ("line", "bus"), split_axis=0, concat_axis=0, tiled=True)
    tags = tags.reshape(owners, n_line, cap).transpose(1, 0, 2).reshape(n_line, owners * cap)
    ordered, rank = order_slots(tags)
    half = owners * cap // 2
    offset = (jnp.arange(n_line, dtype=jnp.int32) * group_buses) % LANES
    before = jnp.minimum((ordered[:, half - 1] + offset) // seg, window // seg - 1)
    after = jnp.minimum((ordered[:, half] + offset) // seg, window // seg)
    after = jnp.where(ordered[:, half] == EMPTY, window // seg, after)
    plan = jnp.stack([before, after])
    picked = select_columns(plan, ordered, transfer_factors, group_buses, window, seg)
    place = lax.axis_index("bus")
    core = (place % 2).reshape(1)
    keep, send = combine(plan, core, rank, arrived, picked, n_bus, n_hours, window // seg, cap)
    other_core = [(i, i ^ 1) for i in range(n_bus)]
    other_chip = [(i, i ^ 2) for i in range(n_bus)]
    summed = keep + lax.ppermute(send, "bus", other_core)
    near = place // 2 == 0
    own = jnp.where(near, summed[0], summed[1])
    away = jnp.where(near, summed[1], summed[0]).astype(jnp.bfloat16)
    return finish(own, lax.ppermute(away, "bus", other_chip), n_lines)


def window_of(group_buses):
    step = math.gcd(group_buses, LANES)
    most = LANES - step + group_buses
    return -(-most // LANES) * LANES


def per_device(*arrays):
    n_line = lax.axis_size("line")
    n_bus = lax.axis_size("bus")
    owners = n_line * n_bus
    n_hours, n_sites = arrays[0].shape
    n_lines, n_columns = arrays[-1].shape
    group_buses = BUSES // owners
    window = window_of(group_buses)
    last = (n_line - 1) * group_buses // LANES * LANES
    fits = (
        n_bus == 4
        and n_hours == 192
        and n_sites == 2 * LANES
        and n_sites * 2 == owners * 16
        and n_line * 16 == LANES
        and n_lines % 16 == 0
        and n_columns % LANES == 0
        and group_buses < EMPTY - LANES
        and window % (3 * LANES) == 0
        and last + window <= n_columns
    )
    if fits:
        return fast_device(*arrays)
    return general_device(*arrays)


def solution(mesh):
    in_specs = (
        P(None, ("line", "bus")),
        P(None, ("line", "bus")),
        P(None, ("line", "bus")),
        P(None, ("line", "bus")),
        P(None, ("line", "bus")),
        P(),
        P(),
        P(("line", "bus")),
        P(("line", "bus")),
        P(),
        P(),
        P(("line", "bus")),
        P(("line", "bus")),
        P("line", "bus"),
    )
    out_specs = P("line", "bus")
    return jax.shard_map(
        per_device, mesh=mesh, in_specs=in_specs, out_specs=out_specs, check_vma=False
    )
```

```python
import functools
import math

import jax
import jax.numpy as jnp
from jax import lax
from jax.experimental import pallas as pl
from jax.experimental.pallas import tpu as pltpu
from jax.sharding import PartitionSpec as P

BUSES = 70144
TILTS = 8
AZIMS = 12


solar_constant = 1367.0
albedo = 0.2
cos_limit = 0.08716
row_width = 36


def pick_table(classes, table, count):
    picked = jnp.zeros(classes.shape, jnp.float32)
    for entry in range(count):
        picked = jnp.where(classes == entry, table[entry], picked)
    return picked


def dirint_lookup(cell, dirint_coef):
    row_count = dirint_coef.shape[0] // row_width
    table = dirint_coef.reshape(row_count, row_width)
    flat_cell = cell.reshape(-1)
    upper = flat_cell // row_width
    lower = flat_cell % row_width
    row_pick = (upper[:, None] == jnp.arange(row_count, dtype=jnp.int32)[None, :]).astype(
        jnp.float32
    )
    rows = jnp.dot(
        row_pick, table, precision=lax.Precision.HIGHEST, preferred_element_type=jnp.float32
    )
    column_hit = lower[:, None] == jnp.arange(row_width, dtype=jnp.int32)[None, :]
    picked = jnp.sum(jnp.where(column_hit, rows, 0.0), axis=1)
    return picked.reshape(cell.shape)


def site_power(
    clear,
    cosz,
    sun_az,
    cell,
    sky,
    tilt_angle,
    array_azimuth,
    site_capacity,
    dirint_coef,
    perez_coef,
):
    global_flat = clear * solar_constant * cosz
    zenith = jnp.arccos(cosz)
    airmass = 1.0 / (cosz + 0.50572 * (96.07995 - zenith * (180.0 / math.pi)) ** (-1.6364))
    clear_beam = (
        0.866 - 0.122 * airmass + 0.0121 * airmass**2 - 0.000653 * airmass**3 + 1.4e-05 * airmass**4
    )
    part_a = 0.512 - 1.56 * clear + 2.286 * clear**2 - 2.222 * clear**3
    part_b = 0.37 + 0.962 * clear
    part_c = -0.28 + 0.932 * clear - 2.048 * clear**2
    beam_index = jnp.maximum(clear_beam - (part_a + part_b * jnp.exp(part_c * airmass)), 0.0)
    direct_normal = solar_constant * beam_index * dirint_lookup(cell, dirint_coef)
    diffuse = jnp.maximum(global_flat - direct_normal * cosz, 0.1 * global_flat)
    brightness = diffuse * airmass / solar_constant
    factors = [jnp.zeros(cosz.shape, jnp.float32) for entry in range(6)]
    for bin_index in range(perez_coef.shape[1]):
        hit = sky == bin_index
        factors = [jnp.where(hit, perez_coef[row, bin_index], factors[row]) for row in range(6)]
    circumsolar = jnp.maximum(0.0, factors[0] + factors[1] * brightness + factors[2] * zenith)
    horizon_term = factors[3] + factors[4] * brightness + factors[5] * zenith
    cos_tilt = jnp.cos(tilt_angle)
    sin_tilt = jnp.sin(tilt_angle)
    cos_incidence = cosz * cos_tilt + jnp.sin(zenith) * sin_tilt * jnp.cos(sun_az - array_azimuth)
    facing = jnp.maximum(cos_incidence, 0.0)
    horizon_cos = jnp.maximum(cosz, cos_limit)
    sky_part = diffuse * (
        (1.0 - circumsolar) * (1.0 + cos_tilt) * 0.5
        + circumsolar * facing / horizon_cos
        + horizon_term * sin_tilt
    )
    plane = direct_normal * facing + sky_part + albedo * global_flat * (1.0 - cos_tilt) * 0.5
    return (site_capacity * plane / 1000.0).astype(jnp.bfloat16)


def general_device(
    clearness,
    cos_zenith,
    sun_azimuth,
    dirint_cell,
    sky_bin,
    dirint_coef,
    perez_coef,
    tilt_class,
    azimuth_class,
    tilt_table,
    azimuth_table,
    capacity,
    site_bus,
    transfer_factors,
):
    line_count = lax.axis_size("line")
    bus_count = lax.axis_size("bus")
    owners = line_count * bus_count
    n_hours, n_sites = clearness.shape
    group_buses = BUSES // owners
    slots_each = max(2, 2 * n_sites // owners)
    tilt_angle = pick_table(tilt_class, tilt_table, TILTS)
    array_azimuth = pick_table(azimuth_class, azimuth_table, AZIMS)
    power = site_power(
        clearness,
        cos_zenith,
        sun_azimuth,
        dirint_cell,
        sky_bin,
        tilt_angle,
        array_azimuth,
        capacity,
        dirint_coef,
        perez_coef,
    )
    group_index = site_bus // group_buses
    target = group_index % line_count * bus_count + group_index // line_count
    local_bus = site_bus % group_buses
    one_hot = (target[:, None] == jnp.arange(owners, dtype=jnp.int32)[None, :]).astype(jnp.int32)
    position = jnp.sum(one_hot * (jnp.cumsum(one_hot, axis=0) - 1), axis=1)
    slot_index = target * slots_each + position
    outgoing = jnp.zeros((n_hours, owners * slots_each), jnp.bfloat16).at[:, slot_index].set(power)
    labels = jnp.zeros((1, owners * slots_each), jnp.int32).at[0, slot_index].set(local_bus)
    arrived, bus_tags = (
        lax.all_to_all(outgoing, ("line", "bus"), split_axis=1, concat_axis=1, tiled=True),
        lax.all_to_all(labels, ("line", "bus"), split_axis=1, concat_axis=1, tiled=True),
    )
    bus_tags = bus_tags.reshape(owners * slots_each)
    member = (bus_tags[:, None] == jnp.arange(group_buses, dtype=jnp.int32)[None, :]).astype(
        jnp.bfloat16
    )
    injection = jnp.einsum("hr,rb->bh", arrived, member, preferred_element_type=jnp.float32).astype(
        jnp.bfloat16
    )
    partial_flows = jnp.dot(
        transfer_factors,
        lax.all_gather(injection, "line", axis=0, tiled=True),
        preferred_element_type=jnp.float32,
    )
    return lax.psum_scatter(partial_flows, "bus", scatter_dimension=1, tiled=True)


LANES = 128
ACOS_POLY = (
    1.5707963262615365,
    -0.21460172591625612,
    0.08904479608150453,
    -0.0507408012983321,
    0.033314914408815,
    -0.02284457168134235,
    0.014575916928409219,
    -0.00744564558483129,
    0.002518626106102872,
    -0.00040427332732297214,
)
COS_POLY = tuple((-1.0) ** k / math.factorial(2 * k) for k in range(8))
SIN_POLY = tuple((-1.0) ** k / math.factorial(2 * k + 1) for k in range(8))
EMPTY = 4095


def horner(x, poly):
    total = jnp.full_like(x, poly[-1])
    for coefficient in poly[-2::-1]:
        total = total * x + coefficient
    return total


def reduce_pi(x):
    turns = jnp.floor(x * (1.0 / math.pi) + 0.5)
    rest = (x - turns * 3.140625) - turns * 0.0009676535897932
    odd = turns - 2.0 * jnp.floor(turns * 0.5)
    return rest, 1.0 - 2.0 * odd


def cosine(x):
    rest, sign = reduce_pi(x)
    return sign * horner(rest * rest, COS_POLY)


def sine(x):
    rest, sign = reduce_pi(x)
    return sign * rest * horner(rest * rest, SIN_POLY)


def to_column(row, eye):
    return jnp.sum(jnp.where(eye, row, 0.0), axis=1, keepdims=True)


def place_kernel(bus_ref, slot_ref, tags_ref, *, owners, group_buses, cap, n_line, n_bus):
    n_sites = bus_ref.shape[1]
    bus = bus_ref[...]
    group = jnp.zeros(bus.shape, jnp.int32)
    for k in range(1, owners):
        group = group + (bus >= k * group_buses).astype(jnp.int32)
    local = (bus - group * group_buses).astype(jnp.float32)
    group = group.astype(jnp.float32)
    first = lax.broadcasted_iota(jnp.int32, (n_sites, n_sites), 0)
    second = lax.broadcasted_iota(jnp.int32, (n_sites, n_sites), 1)
    eye = first == second
    earlier = (to_column(group, eye) == group) & (first < second)
    position = jnp.sum(jnp.where(earlier, 1.0, 0.0), axis=0, keepdims=True)
    slot = group * float(cap) + position
    slot_ref[...] = slot.astype(jnp.int32)
    slot_column = to_column(slot, eye).astype(jnp.int32)
    local_column = to_column(local, eye)
    n_slots = n_line * cap
    for bus_index in range(n_bus):
        lanes = lax.broadcasted_iota(jnp.int32, (n_sites, n_slots), 1) + bus_index * n_slots
        hit = slot_column == lanes
        tag = jnp.sum(jnp.where(hit, local_column + 1.0, 0.0), axis=0, keepdims=True)
        tag = jnp.where(tag > 0.5, tag - 1.0, float(EMPTY)).astype(jnp.int32)
        for line_index in range(n_line):
            row = line_index * n_bus + bus_index
            tags_ref[row : row + 1, :] = tag


def place_sites(site_bus, owners, group_buses, cap, n_line, n_bus):
    n_sites = site_bus.shape[0]
    return pl.pallas_call(
        functools.partial(
            place_kernel,
            owners=owners,
            group_buses=group_buses,
            cap=cap,
            n_line=n_line,
            n_bus=n_bus,
        ),
        out_shape=(
            jax.ShapeDtypeStruct((1, n_sites), jnp.int32),
            jax.ShapeDtypeStruct((owners, n_line * cap), jnp.int32),
        ),
        cost_estimate=pl.CostEstimate(flops=10**6, bytes_accessed=10**5, transcendentals=0),
        name="place",
    )(site_bus.reshape(1, n_sites))


def power_kernel(
    tilt_table_ref,
    azimuth_table_ref,
    *refs,
    n_line,
    n_bus,
    cap,
    rows,
):
    sources = refs[:11]
    out_ref = refs[11]
    held = refs[12:23]
    power_ref, dirint_rows, perez_rows, sems = refs[23:]
    copies = [
        pltpu.make_async_copy(source, place, sems.at[i])
        for i, (source, place) in enumerate(zip(sources, held))
    ]
    for copy in copies:
        copy.start()
    for copy in copies:
        copy.wait()
    clear_all, cosz_all, sun_all, cell_all, sky_all = held[:5]
    dirint_ref, perez_ref, tilt_class_ref, azimuth_class_ref, capacity_ref, slot_ref = held[5:]
    n_hours, n_sites = clear_all.shape
    cells = dirint_ref.shape[1]
    dirint_rows[...] = jnp.zeros_like(dirint_rows)
    dirint_rows[:, :cells] = dirint_ref[...]
    perez_rows[...] = jnp.zeros_like(perez_rows)
    perez_rows[: perez_ref.shape[0], : perez_ref.shape[1]] = perez_ref[...]
    tilt_class = tilt_class_ref[...]
    azimuth_class = azimuth_class_ref[...]
    tilt = jnp.zeros(tilt_class.shape, jnp.float32)
    for entry in range(TILTS):
        tilt = jnp.where(tilt_class == entry, tilt_table_ref[entry], tilt)
    azimuth = jnp.zeros(tilt_class.shape, jnp.float32)
    for entry in range(AZIMS):
        azimuth = jnp.where(azimuth_class == entry, azimuth_table_ref[entry], azimuth)
    wide = (rows, LANES)
    cos_tilts = cosine(tilt)
    sin_tilts = sine(tilt)
    capacity = capacity_ref[...]

    def some_hours(now, carry):
        at = pl.ds(pl.multiple_of(now * rows, rows), rows)
        for part in range(n_sites // LANES):
            lanes = slice(part * LANES, (part + 1) * LANES)
            cos_tilt = jnp.broadcast_to(cos_tilts[:, lanes], wide)
            sin_tilt = jnp.broadcast_to(sin_tilts[:, lanes], wide)
            array_azimuth = jnp.broadcast_to(azimuth[:, lanes], wide)
            site_capacity = jnp.broadcast_to(capacity[:, lanes], wide)
            clear = clear_all[at, lanes]
            cosz = cosz_all[at, lanes]
            sun_az = sun_all[at, lanes]
            cell = cell_all[at, lanes]
            sky = sky_all[at, lanes]
            global_flat = clear * solar_constant * cosz
            zenith = jnp.sqrt(1.0 - cosz) * horner(cosz, ACOS_POLY)
            sin_zenith = jnp.sqrt((1.0 - cosz) * (1.0 + cosz))
            height = 96.07995 - zenith * (180.0 / math.pi)
            airmass = 1.0 / (cosz + 0.50572 * jnp.exp(-1.6364 * jnp.log(height)))
            clear_beam = horner(airmass, (0.866, -0.122, 0.0121, -0.000653, 1.4e-05))
            part_a = horner(clear, (0.512, -1.56, 2.286, -2.222))
            part_b = 0.37 + 0.962 * clear
            part_c = horner(clear, (-0.28, 0.932, -2.048))
            beam = jnp.maximum(clear_beam - (part_a + part_b * jnp.exp(part_c * airmass)), 0.0)
            low = cell & (LANES - 1)
            high = cell >> 7
            coefficient = jnp.zeros(wide, jnp.float32)
            for row in range(dirint_rows.shape[1] // LANES):
                line = dirint_rows[:, row * LANES : (row + 1) * LANES]
                found = jnp.take_along_axis(
                    jnp.broadcast_to(line, wide), low, axis=1, mode="promise_in_bounds"
                )
                coefficient = jnp.where(high == row, found, coefficient)
            direct = solar_constant * beam * coefficient
            diffuse = jnp.maximum(global_flat - direct * cosz, 0.1 * global_flat)
            bright = diffuse * airmass * (1.0 / solar_constant)
            factor = [
                jnp.take_along_axis(
                    jnp.broadcast_to(perez_rows[row : row + 1, :], wide),
                    sky,
                    axis=1,
                    mode="promise_in_bounds",
                )
                for row in range(6)
            ]
            circumsolar = jnp.maximum(0.0, factor[0] + factor[1] * bright + factor[2] * zenith)
            horizon = factor[3] + factor[4] * bright + factor[5] * zenith
            facing = jnp.maximum(
                cosz * cos_tilt + sin_zenith * sin_tilt * cosine(sun_az - array_azimuth), 0.0
            )
            sky_part = diffuse * (
                (1.0 - circumsolar) * (1.0 + cos_tilt) * 0.5
                + circumsolar * facing / jnp.maximum(cosz, cos_limit)
                + horizon * sin_tilt
            )
            plane = direct * facing + sky_part + albedo * global_flat * (1.0 - cos_tilt) * 0.5
            power_ref[at, lanes] = (site_capacity * plane / 1000.0).astype(jnp.bfloat16)
        return carry

    lax.fori_loop(0, n_hours // rows, some_hours, 0)
    power = power_ref[...]
    low_hours = power[:LANES]
    rest = power[LANES:]
    blank = jnp.zeros_like(rest)
    left = jnp.concatenate([rest, blank], axis=0)
    right = jnp.concatenate([blank, rest], axis=0)
    slot = slot_ref[...]
    n_slots = n_line * cap
    half = cap // 2
    dims = (((1,), (1,)), ((), ()))
    for bus_index in range(n_bus):
        base = bus_index * n_slots
        slots = lax.broadcasted_iota(jnp.int32, (n_slots, n_sites), 0) + base
        pick = jnp.where(slots == slot, 1.0, 0.0).astype(jnp.bfloat16)
        top = lax.dot_general(pick, low_hours, dims, preferred_element_type=jnp.float32)
        index = lax.broadcasted_iota(jnp.int32, (n_slots // 2, n_sites), 0)
        paired = (index // half) * cap + index % half + base
        pick_left = jnp.where(paired == slot, 1.0, 0.0).astype(jnp.bfloat16)
        pick_right = jnp.where(paired + half == slot, 1.0, 0.0).astype(jnp.bfloat16)
        bottom = lax.dot_general(
            pick_left, left, dims, preferred_element_type=jnp.float32
        ) + lax.dot_general(pick_right, right, dims, preferred_element_type=jnp.float32)
        top = top.astype(jnp.bfloat16)
        bottom = bottom.astype(jnp.bfloat16)
        for line_index in range(n_line):
            row = line_index * n_bus + bus_index
            out_ref[row, :n_slots, :] = top
            out_ref[row, n_slots:, :] = bottom


def packed_power(
    tilt_table,
    azimuth_table,
    hourly,
    dirint_coef,
    perez_coef,
    tilt_class,
    azimuth_class,
    capacity,
    slot,
    n_line,
    n_bus,
    cap,
):
    n_hours, n_sites = hourly[0].shape
    owners = n_line * n_bus
    n_slots = n_line * cap
    cells = dirint_coef.shape[0]
    rows = 32
    smem = pl.BlockSpec(memory_space=pltpu.SMEM)
    shape = (owners, n_slots * n_hours // LANES, LANES)
    operands = (
        *hourly,
        dirint_coef.reshape(1, cells),
        perez_coef,
        tilt_class.reshape(1, n_sites),
        azimuth_class.reshape(1, n_sites),
        capacity.reshape(1, n_sites),
        slot,
    )
    return pl.pallas_call(
        functools.partial(power_kernel, n_line=n_line, n_bus=n_bus, cap=cap, rows=rows),
        out_shape=jax.ShapeDtypeStruct(shape, jnp.bfloat16),
        in_specs=[smem, smem] + [pl.BlockSpec(memory_space=pltpu.HBM)] * len(operands),
        out_specs=pl.BlockSpec(memory_space=pltpu.VMEM),
        scratch_shapes=[pltpu.VMEM(x.shape, x.dtype) for x in operands]
        + [
            pltpu.VMEM((n_hours, n_sites), jnp.bfloat16),
            pltpu.VMEM((1, -(-cells // LANES) * LANES), jnp.float32),
            pltpu.VMEM((8, LANES), jnp.float32),
            pltpu.SemaphoreType.DMA((len(operands),)),
        ],
        compiler_params=pltpu.CompilerParams(vmem_limit_bytes=64 << 20),
        cost_estimate=pl.CostEstimate(
            flops=2 * 10**8, bytes_accessed=3 * 10**6, transcendentals=2 * 10**5
        ),
        name="power",
    )(tilt_table, azimuth_table, *operands)


def order_slots(tags_ref, sorted_ref, rank_ref, plan_ref, group_buses):
    n_groups, n_slots = tags_ref.shape
    half = n_slots // 2
    tags = tags_ref[...].astype(jnp.float32)
    lanes = lax.broadcasted_iota(jnp.int32, (n_slots, n_slots), 1).astype(jnp.float32)
    index = lax.broadcasted_iota(jnp.int32, (n_groups, n_slots), 1)
    keys = tags * n_slots + index.astype(jnp.float32)
    tag_columns = jnp.transpose(tags)
    key_columns = jnp.transpose(keys)
    ranks = []
    for g in range(n_groups):
        smaller = key_columns[:, g : g + 1] < keys[g : g + 1]
        ranks.append(jnp.sum(jnp.where(smaller, 1.0, 0.0), axis=0, keepdims=True))
    rank = jnp.concatenate(ranks, axis=0)
    rank_ref[...] = rank.astype(jnp.int32)
    rank_columns = jnp.transpose(rank)
    ordered = []
    for g in range(n_groups):
        hit = rank_columns[:, g : g + 1] == lanes
        found = jnp.sum(jnp.where(hit, tag_columns[:, g : g + 1], 0.0), axis=0, keepdims=True)
        ordered.append(found + float(g * group_buses % LANES))
    ordered = jnp.concatenate(ordered, axis=0)
    sorted_ref[...] = ordered.astype(jnp.int32)
    real = ordered < float(EMPTY)
    last = jnp.max(jnp.where(real & (index < half), ordered, 0.0), axis=1, keepdims=True)
    after = jnp.min(jnp.where(real & (index >= half), ordered, 2.0 * EMPTY), axis=1, keepdims=True)
    for g in range(n_groups):
        plan_ref[0, g] = jnp.max(last[g : g + 1]).astype(jnp.int32)
        plan_ref[1, g] = jnp.max(after[g : g + 1]).astype(jnp.int32)


def select_kernel(
    tags_ref,
    factors_ref,
    out_ref,
    rank_ref,
    buffer,
    pick,
    sorted_ref,
    plan_ref,
    sems,
    *,
    group_buses,
    window,
    seg,
):
    g = pl.program_id(0)
    n_groups = pl.num_programs(0)
    n_slots = out_ref.shape[1]
    half = n_slots // 2
    n_seg = window // seg

    def copy(index):
        start = pl.multiple_of((index * group_buses) // LANES * LANES, LANES)
        slot = lax.rem(index, 2)
        return pltpu.make_async_copy(
            factors_ref.at[:, pl.ds(start, window)], buffer.at[slot], sems.at[slot]
        )

    @pl.when(g == 0)
    def _():
        copy(g).start()

    @pl.when(g + 1 < n_groups)
    def _():
        copy(g + 1).start()

    @pl.when(g == 0)
    def _():
        order_slots(tags_ref, sorted_ref, rank_ref, plan_ref, group_buses)

    last = plan_ref[0, g]
    after = plan_ref[1, g]
    place = sorted_ref[pl.ds(g, 1), :]

    def wanted(chunk, k):
        if chunk == 0:
            return last >= k * seg
        return after < (k + 1) * seg

    for chunk in range(2):
        columns = slice(chunk * half, (chunk + 1) * half)
        for k in range(n_seg):

            @pl.when(wanted(chunk, k))
            def _():
                buses = lax.broadcasted_iota(jnp.int32, (seg, half), 0) + k * seg
                pick[k * seg : (k + 1) * seg, columns] = jnp.where(
                    buses == place[:, columns], 1.0, 0.0
                ).astype(jnp.bfloat16)

    copy(g).wait()
    now = lax.rem(g, 2)
    for k in range(n_seg):
        stop = (k + 1) * seg
        begin = k * seg
        ends_here = last < stop if k + 1 < n_seg else last >= begin
        if 0 < k < n_seg - 1:
            ends_here = ends_here & (last >= begin)

        @pl.when(ends_here)
        def _():
            out_ref[:, :half] = jnp.dot(
                buffer[now, :, :stop], pick[:stop, :half], preferred_element_type=jnp.float32
            ).astype(jnp.bfloat16)

        starts_here = after < stop
        if k:
            starts_here = starts_here & (after >= begin)

        @pl.when(starts_here)
        def _():
            out_ref[:, half:] = jnp.dot(
                buffer[now, :, begin:], pick[begin:, half:], preferred_element_type=jnp.float32
            ).astype(jnp.bfloat16)

    @pl.when(after >= window)
    def _():
        out_ref[:, half:] = jnp.zeros((out_ref.shape[0], half), jnp.bfloat16)


def select_columns(tags, factors, group_buses, window, seg):
    n_groups, n_slots = tags.shape
    n_lines = factors.shape[0]
    whole = pl.BlockSpec((n_groups, n_slots), lambda g: (0, 0))
    return pl.pallas_call(
        functools.partial(select_kernel, group_buses=group_buses, window=window, seg=seg),
        grid=(n_groups,),
        in_specs=[whole, pl.BlockSpec(memory_space=pltpu.HBM)],
        out_specs=(pl.BlockSpec((n_lines, n_slots), lambda g: (0, g)), whole),
        out_shape=(
            jax.ShapeDtypeStruct((n_lines, n_groups * n_slots), jnp.bfloat16),
            jax.ShapeDtypeStruct((n_groups, n_slots), jnp.int32),
        ),
        scratch_shapes=[
            pltpu.VMEM((2, n_lines, window), jnp.bfloat16),
            pltpu.VMEM((window, n_slots), jnp.bfloat16),
            pltpu.VMEM((n_groups, n_slots), jnp.int32),
            pltpu.SMEM((2, n_groups), jnp.int32),
            pltpu.SemaphoreType.DMA((2,)),
        ],
        compiler_params=pltpu.CompilerParams(vmem_limit_bytes=48 << 20),
        cost_estimate=pl.CostEstimate(
            flops=2 * n_lines * window * n_groups * n_slots,
            bytes_accessed=2 * n_lines * window * n_groups,
            transcendentals=0,
        ),
        name="select",
    )(tags, factors)


def move_power(rank_ref, arrived_ref, moved_ref, cap):
    n_groups, n_slots = rank_ref.shape
    half = cap // 2
    tops = n_groups * cap
    places = lax.broadcasted_iota(jnp.int32, (n_slots, n_slots), 0)
    for g in range(n_groups):
        top = arrived_ref[:, g * cap : (g + 1) * cap, :].reshape(n_slots, LANES)
        bottom = arrived_ref[:, tops + g * half : tops + (g + 1) * half, :].astype(jnp.float32)
        blocks = bottom.shape[0]
        turned = pltpu.roll(bottom.reshape(blocks * half, LANES), LANES // 2, 1)
        bottom = jnp.concatenate([bottom, turned.reshape(blocks, half, LANES)], axis=1)
        bottom = bottom.reshape(n_slots, LANES).astype(jnp.bfloat16)
        power = jnp.concatenate([top, bottom], axis=1)
        move = jnp.where(places == rank_ref[g : g + 1, :], 1.0, 0.0).astype(jnp.bfloat16)
        moved = jnp.dot(move, power, preferred_element_type=jnp.float32)
        moved_ref[g * n_slots : (g + 1) * n_slots, :] = moved.astype(jnp.bfloat16)


def lines_kernel(
    core_ref, rank_ref, arrived_ref, picked_ref, keep_a, send_a, keep_b, send_b, moved_ref, *, cap, first
):
    step = pl.program_id(0)

    @pl.when(step == 0)
    def _():
        move_power(rank_ref, arrived_ref, moved_ref, cap)

    flow = jnp.dot(picked_ref[...], moved_ref[...], preferred_element_type=jnp.float32)
    turned = jnp.transpose(flow)
    rows_each = keep_a.shape[1]
    core_zero = core_ref[0] == 0
    keep = []
    send = []
    for x in range(keep_a.shape[0]):
        begin = 2 * x * rows_each
        even = turned[begin : begin + rows_each]
        odd = turned[begin + rows_each : begin + 2 * rows_each]
        keep.append(jnp.where(core_zero, even, odd))
        send.append(jnp.where(core_zero, odd, even))

    def write(keep_ref, send_ref):
        for x in range(keep_ref.shape[0]):
            keep_ref[x] = keep[x]
            send_ref[x] = send[x]

    @pl.when(step < first)
    def _():
        write(keep_a, send_a)

    @pl.when(step >= first)
    def _():
        write(keep_b, send_b)


def lines(core, rank, arrived, picked, n_bus, n_hours, cap, block):
    n_groups, n_slots = rank.shape
    n_lines = picked.shape[0]
    steps = -(-n_lines // block)
    first = -(-steps // 2)
    shape = (n_bus // 2, n_hours // n_bus)

    def early(i):
        return (0, 0, jnp.minimum(i, first - 1))

    def late(i):
        return (0, 0, jnp.maximum(i - first, 0))

    blocks = [pl.BlockSpec(shape + (block,), early)] * 2 + [pl.BlockSpec(shape + (block,), late)] * 2
    counts = [first * block] * 2 + [(steps - first) * block] * 2
    return pl.pallas_call(
        functools.partial(lines_kernel, cap=cap, first=first),
        grid=(steps,),
        in_specs=[
            pl.BlockSpec(memory_space=pltpu.SMEM),
            pl.BlockSpec(rank.shape, lambda i: (0, 0)),
            pl.BlockSpec(arrived.shape, lambda i: (0, 0, 0)),
            pl.BlockSpec((block, picked.shape[1]), lambda i: (i, 0)),
        ],
        out_specs=blocks,
        out_shape=[jax.ShapeDtypeStruct(shape + (count,), jnp.float32) for count in counts],
        scratch_shapes=[pltpu.VMEM((n_groups * n_slots, 2 * LANES), jnp.bfloat16)],
        compiler_params=pltpu.CompilerParams(vmem_limit_bytes=40 << 20),
        cost_estimate=pl.CostEstimate(
            flops=4 * n_lines * n_groups * n_slots * LANES,
            bytes_accessed=2 * n_lines * n_groups * n_slots,
            transcendentals=0,
        ),
        name="lines",
    )(core, rank, arrived, picked)


def finish_kernel(*refs):
    out_ref = refs[-1]
    parts = refs[:-1]
    begin = 0
    for i in range(len(parts) // 2):
        total = parts[2 * i][...] + parts[2 * i + 1][...].astype(jnp.float32)
        count = min(total.shape[1], out_ref.shape[1] - begin)
        out_ref[:, begin : begin + count] = total[:, :count]
        begin += count


def finish(parts, n_lines):
    rows = parts[0].shape[0]
    return pl.pallas_call(
        finish_kernel,
        in_specs=[pl.BlockSpec(memory_space=pltpu.VMEM)] * len(parts),
        out_specs=pl.BlockSpec(memory_space=pltpu.VMEM),
        out_shape=jax.ShapeDtypeStruct((rows, n_lines), jnp.float32),
        compiler_params=pltpu.CompilerParams(vmem_limit_bytes=64 << 20),
        cost_estimate=pl.CostEstimate(
            flops=n_lines * rows, bytes_accessed=12 * n_lines * rows, transcendentals=0
        ),
        name="finish",
    )(*parts)


def fast_device(
    clearness,
    cos_zenith,
    sun_azimuth,
    dirint_cell,
    sky_bin,
    dirint_coef,
    perez_coef,
    tilt_class,
    azimuth_class,
    tilt_table,
    azimuth_table,
    capacity,
    site_bus,
    transfer_factors,
):
    n_line = lax.axis_size("line")
    n_bus = lax.axis_size("bus")
    owners = n_line * n_bus
    n_hours, n_sites = clearness.shape
    n_lines, n_columns = transfer_factors.shape
    group_buses = BUSES // owners
    cap = 2 * n_sites // owners
    window = window_of(group_buses)
    seg = window // 3
    slot, tags = place_sites(site_bus, owners, group_buses, cap, n_line, n_bus)
    tags = lax.all_to_all(tags, ("line", "bus"), split_axis=0, concat_axis=0, tiled=True)
    outgoing = packed_power(
        tilt_table,
        azimuth_table,
        (clearness, cos_zenith, sun_azimuth, dirint_cell, sky_bin),
        dirint_coef,
        perez_coef,
        tilt_class,
        azimuth_class,
        capacity,
        slot,
        n_line,
        n_bus,
        cap,
    )
    arrived = lax.all_to_all(outgoing, ("line", "bus"), split_axis=0, concat_axis=0, tiled=True)
    tags = tags.reshape(owners, n_line, cap).transpose(1, 0, 2).reshape(n_line, owners * cap)
    picked, rank = select_columns(tags, transfer_factors, group_buses, window, seg)
    place = lax.axis_index("bus")
    core = (place % 2).reshape(1)
    near = place // 2 == 0
    other_core = [(i, i ^ 1) for i in range(n_bus)]
    other_chip = [(i, i ^ 2) for i in range(n_bus)]
    keep_a, send_a, keep_b, send_b = lines(
        core, rank, arrived, picked, n_bus, n_hours, cap, 512
    )
    ends = []
    for keep, send in ((keep_a, send_a), (keep_b, send_b)):
        summed = keep + lax.ppermute(send, "bus", other_core)
        own = jnp.where(near, summed[0], summed[1])
        away = jnp.where(near, summed[1], summed[0]).astype(jnp.bfloat16)
        away = lax.ppermute(away, "bus", other_chip)
        ends += [own, away]
    return finish(ends, n_lines).T


def window_of(group_buses):
    step = math.gcd(group_buses, LANES)
    most = LANES - step + group_buses
    return -(-most // LANES) * LANES


def per_device(*arrays):
    n_line = lax.axis_size("line")
    n_bus = lax.axis_size("bus")
    owners = n_line * n_bus
    n_hours, n_sites = arrays[0].shape
    n_lines, n_columns = arrays[-1].shape
    group_buses = BUSES // owners
    window = window_of(group_buses)
    last = (n_line - 1) * group_buses // LANES * LANES
    fits = (
        n_bus == 4
        and n_hours == 192
        and n_sites == 2 * LANES
        and n_sites * 2 == owners * 16
        and n_line * 16 == LANES
        and n_lines % 16 == 0
        and n_columns % LANES == 0
        and group_buses < EMPTY - LANES
        and window % (3 * LANES) == 0
        and last + window <= n_columns
    )
    if fits:
        return fast_device(*arrays)
    return general_device(*arrays)


def solution(mesh):
    in_specs = (
        P(None, ("line", "bus")),
        P(None, ("line", "bus")),
        P(None, ("line", "bus")),
        P(None, ("line", "bus")),
        P(None, ("line", "bus")),
        P(),
        P(),
        P(("line", "bus")),
        P(("line", "bus")),
        P(),
        P(),
        P(("line", "bus")),
        P(("line", "bus")),
        P("line", "bus"),
    )
    out_specs = P("line", "bus")
    return jax.shard_map(
        per_device, mesh=mesh, in_specs=in_specs, out_specs=out_specs, check_vma=False
    )
```

```python
import functools
import math

import jax
import jax.numpy as jnp
from jax import lax
from jax.experimental import pallas as pl
from jax.experimental.pallas import tpu as pltpu
from jax.sharding import PartitionSpec as P

BUSES = 70144
TILTS = 8
AZIMS = 12


solar_constant = 1367.0
albedo = 0.2
cos_limit = 0.08716
row_width = 36


def pick_table(classes, table, count):
    picked = jnp.zeros(classes.shape, jnp.float32)
    for entry in range(count):
        picked = jnp.where(classes == entry, table[entry], picked)
    return picked


def dirint_lookup(cell, dirint_coef):
    row_count = dirint_coef.shape[0] // row_width
    table = dirint_coef.reshape(row_count, row_width)
    flat_cell = cell.reshape(-1)
    upper = flat_cell // row_width
    lower = flat_cell % row_width
    row_pick = (upper[:, None] == jnp.arange(row_count, dtype=jnp.int32)[None, :]).astype(
        jnp.float32
    )
    rows = jnp.dot(
        row_pick, table, precision=lax.Precision.HIGHEST, preferred_element_type=jnp.float32
    )
    column_hit = lower[:, None] == jnp.arange(row_width, dtype=jnp.int32)[None, :]
    picked = jnp.sum(jnp.where(column_hit, rows, 0.0), axis=1)
    return picked.reshape(cell.shape)


def site_power(
    clear,
    cosz,
    sun_az,
    cell,
    sky,
    tilt_angle,
    array_azimuth,
    site_capacity,
    dirint_coef,
    perez_coef,
):
    global_flat = clear * solar_constant * cosz
    zenith = jnp.arccos(cosz)
    airmass = 1.0 / (cosz + 0.50572 * (96.07995 - zenith * (180.0 / math.pi)) ** (-1.6364))
    clear_beam = (
        0.866 - 0.122 * airmass + 0.0121 * airmass**2 - 0.000653 * airmass**3 + 1.4e-05 * airmass**4
    )
    part_a = 0.512 - 1.56 * clear + 2.286 * clear**2 - 2.222 * clear**3
    part_b = 0.37 + 0.962 * clear
    part_c = -0.28 + 0.932 * clear - 2.048 * clear**2
    beam_index = jnp.maximum(clear_beam - (part_a + part_b * jnp.exp(part_c * airmass)), 0.0)
    direct_normal = solar_constant * beam_index * dirint_lookup(cell, dirint_coef)
    diffuse = jnp.maximum(global_flat - direct_normal * cosz, 0.1 * global_flat)
    brightness = diffuse * airmass / solar_constant
    factors = [jnp.zeros(cosz.shape, jnp.float32) for entry in range(6)]
    for bin_index in range(perez_coef.shape[1]):
        hit = sky == bin_index
        factors = [jnp.where(hit, perez_coef[row, bin_index], factors[row]) for row in range(6)]
    circumsolar = jnp.maximum(0.0, factors[0] + factors[1] * brightness + factors[2] * zenith)
    horizon_term = factors[3] + factors[4] * brightness + factors[5] * zenith
    cos_tilt = jnp.cos(tilt_angle)
    sin_tilt = jnp.sin(tilt_angle)
    cos_incidence = cosz * cos_tilt + jnp.sin(zenith) * sin_tilt * jnp.cos(sun_az - array_azimuth)
    facing = jnp.maximum(cos_incidence, 0.0)
    horizon_cos = jnp.maximum(cosz, cos_limit)
    sky_part = diffuse * (
        (1.0 - circumsolar) * (1.0 + cos_tilt) * 0.5
        + circumsolar * facing / horizon_cos
        + horizon_term * sin_tilt
    )
    plane = direct_normal * facing + sky_part + albedo * global_flat * (1.0 - cos_tilt) * 0.5
    return (site_capacity * plane / 1000.0).astype(jnp.bfloat16)


def general_device(
    clearness,
    cos_zenith,
    sun_azimuth,
    dirint_cell,
    sky_bin,
    dirint_coef,
    perez_coef,
    tilt_class,
    azimuth_class,
    tilt_table,
    azimuth_table,
    capacity,
    site_bus,
    transfer_factors,
):
    line_count = lax.axis_size("line")
    bus_count = lax.axis_size("bus")
    owners = line_count * bus_count
    n_hours, n_sites = clearness.shape
    group_buses = BUSES // owners
    slots_each = max(2, 2 * n_sites // owners)
    tilt_angle = pick_table(tilt_class, tilt_table, TILTS)
    array_azimuth = pick_table(azimuth_class, azimuth_table, AZIMS)
    power = site_power(
        clearness,
        cos_zenith,
        sun_azimuth,
        dirint_cell,
        sky_bin,
        tilt_angle,
        array_azimuth,
        capacity,
        dirint_coef,
        perez_coef,
    )
    group_index = site_bus // group_buses
    target = group_index % line_count * bus_count + group_index // line_count
    local_bus = site_bus % group_buses
    one_hot = (target[:, None] == jnp.arange(owners, dtype=jnp.int32)[None, :]).astype(jnp.int32)
    position = jnp.sum(one_hot * (jnp.cumsum(one_hot, axis=0) - 1), axis=1)
    slot_index = target * slots_each + position
    outgoing = jnp.zeros((n_hours, owners * slots_each), jnp.bfloat16).at[:, slot_index].set(power)
    labels = jnp.zeros((1, owners * slots_each), jnp.int32).at[0, slot_index].set(local_bus)
    arrived, bus_tags = (
        lax.all_to_all(outgoing, ("line", "bus"), split_axis=1, concat_axis=1, tiled=True),
        lax.all_to_all(labels, ("line", "bus"), split_axis=1, concat_axis=1, tiled=True),
    )
    bus_tags = bus_tags.reshape(owners * slots_each)
    member = (bus_tags[:, None] == jnp.arange(group_buses, dtype=jnp.int32)[None, :]).astype(
        jnp.bfloat16
    )
    injection = jnp.einsum("hr,rb->bh", arrived, member, preferred_element_type=jnp.float32).astype(
        jnp.bfloat16
    )
    partial_flows = jnp.dot(
        transfer_factors,
        lax.all_gather(injection, "line", axis=0, tiled=True),
        preferred_element_type=jnp.float32,
    )
    return lax.psum_scatter(partial_flows, "bus", scatter_dimension=1, tiled=True)


LANES = 128
ACOS_POLY = (
    1.5707963262615365,
    -0.21460172591625612,
    0.08904479608150453,
    -0.0507408012983321,
    0.033314914408815,
    -0.02284457168134235,
    0.014575916928409219,
    -0.00744564558483129,
    0.002518626106102872,
    -0.00040427332732297214,
)
COS_POLY = tuple((-1.0) ** k / math.factorial(2 * k) for k in range(8))
SIN_POLY = tuple((-1.0) ** k / math.factorial(2 * k + 1) for k in range(8))
EMPTY = 4095


def horner(x, poly):
    total = jnp.full_like(x, poly[-1])
    for coefficient in poly[-2::-1]:
        total = total * x + coefficient
    return total


def reduce_pi(x):
    turns = jnp.floor(x * (1.0 / math.pi) + 0.5)
    rest = (x - turns * 3.140625) - turns * 0.0009676535897932
    odd = turns - 2.0 * jnp.floor(turns * 0.5)
    return rest, 1.0 - 2.0 * odd


def cosine(x):
    rest, sign = reduce_pi(x)
    return sign * horner(rest * rest, COS_POLY)


def sine(x):
    rest, sign = reduce_pi(x)
    return sign * rest * horner(rest * rest, SIN_POLY)


def to_column(row, eye):
    return jnp.sum(jnp.where(eye, row, 0.0), axis=1, keepdims=True)


def place_kernel(bus_ref, slot_ref, tags_ref, *, owners, group_buses, cap, n_line, n_bus):
    n_sites = bus_ref.shape[1]
    bus = bus_ref[...]
    group = jnp.zeros(bus.shape, jnp.int32)
    for k in range(1, owners):
        group = group + (bus >= k * group_buses).astype(jnp.int32)
    local = (bus - group * group_buses).astype(jnp.float32)
    group = group.astype(jnp.float32)
    first = lax.broadcasted_iota(jnp.int32, (n_sites, n_sites), 0)
    second = lax.broadcasted_iota(jnp.int32, (n_sites, n_sites), 1)
    eye = first == second
    earlier = (to_column(group, eye) == group) & (first < second)
    position = jnp.sum(jnp.where(earlier, 1.0, 0.0), axis=0, keepdims=True)
    slot = group * float(cap) + position
    slot_ref[...] = slot.astype(jnp.int32)
    slot_column = to_column(slot, eye).astype(jnp.int32)
    local_column = to_column(local, eye)
    n_slots = n_line * cap
    for bus_index in range(n_bus):
        lanes = lax.broadcasted_iota(jnp.int32, (n_sites, n_slots), 1) + bus_index * n_slots
        hit = slot_column == lanes
        tag = jnp.sum(jnp.where(hit, local_column + 1.0, 0.0), axis=0, keepdims=True)
        tag = jnp.where(tag > 0.5, tag - 1.0, float(EMPTY)).astype(jnp.int32)
        for line_index in range(n_line):
            row = line_index * n_bus + bus_index
            tags_ref[row : row + 1, :] = tag


def place_sites(site_bus, owners, group_buses, cap, n_line, n_bus):
    n_sites = site_bus.shape[0]
    return pl.pallas_call(
        functools.partial(
            place_kernel,
            owners=owners,
            group_buses=group_buses,
            cap=cap,
            n_line=n_line,
            n_bus=n_bus,
        ),
        out_shape=(
            jax.ShapeDtypeStruct((1, n_sites), jnp.int32),
            jax.ShapeDtypeStruct((owners, n_line * cap), jnp.int32),
        ),
        cost_estimate=pl.CostEstimate(flops=10**6, bytes_accessed=10**5, transcendentals=0),
        name="place",
    )(site_bus.reshape(1, n_sites))


def power_kernel(
    tilt_table_ref,
    azimuth_table_ref,
    *refs,
    n_line,
    n_bus,
    cap,
    rows,
):
    sources = refs[:11]
    out_ref = refs[11]
    held = refs[12:23]
    power_ref, dirint_rows, perez_rows, sems = refs[23:]
    copies = [
        pltpu.make_async_copy(source, place, sems.at[i])
        for i, (source, place) in enumerate(zip(sources, held))
    ]
    for copy in copies:
        copy.start()
    for copy in copies:
        copy.wait()
    clear_all, cosz_all, sun_all, cell_all, sky_all = held[:5]
    dirint_ref, perez_ref, tilt_class_ref, azimuth_class_ref, capacity_ref, slot_ref = held[5:]
    n_hours, n_sites = clear_all.shape
    cells = dirint_ref.shape[0]
    dirint_rows[...] = jnp.zeros_like(dirint_rows)
    for begin in range(0, cells, LANES):
        count = min(LANES, cells - begin)
        dirint_rows[:, begin : begin + count] = dirint_ref[begin : begin + count].reshape(1, count)
    perez_rows[...] = jnp.zeros_like(perez_rows)
    perez_rows[: perez_ref.shape[0], : perez_ref.shape[1]] = perez_ref[...]
    tilt_class = tilt_class_ref[...]
    azimuth_class = azimuth_class_ref[...]
    tilt = jnp.zeros(tilt_class.shape, jnp.float32)
    for entry in range(TILTS):
        tilt = jnp.where(tilt_class == entry, tilt_table_ref[entry], tilt)
    azimuth = jnp.zeros(tilt_class.shape, jnp.float32)
    for entry in range(AZIMS):
        azimuth = jnp.where(azimuth_class == entry, azimuth_table_ref[entry], azimuth)
    wide = (rows, LANES)
    cos_tilts = cosine(tilt)
    sin_tilts = sine(tilt)
    capacity = capacity_ref[...]

    def some_hours(now, carry):
        at = pl.ds(pl.multiple_of(now * rows, rows), rows)
        for part in range(n_sites // LANES):
            lanes = slice(part * LANES, (part + 1) * LANES)
            cos_tilt = jnp.broadcast_to(cos_tilts[:, lanes], wide)
            sin_tilt = jnp.broadcast_to(sin_tilts[:, lanes], wide)
            array_azimuth = jnp.broadcast_to(azimuth[:, lanes], wide)
            site_capacity = jnp.broadcast_to(capacity[:, lanes], wide)
            clear = clear_all[at, lanes]
            cosz = cosz_all[at, lanes]
            sun_az = sun_all[at, lanes]
            cell = cell_all[at, lanes]
            sky = sky_all[at, lanes]
            global_flat = clear * solar_constant * cosz
            zenith = jnp.sqrt(1.0 - cosz) * horner(cosz, ACOS_POLY)
            sin_zenith = jnp.sqrt((1.0 - cosz) * (1.0 + cosz))
            height = 96.07995 - zenith * (180.0 / math.pi)
            airmass = 1.0 / (cosz + 0.50572 * jnp.exp(-1.6364 * jnp.log(height)))
            clear_beam = horner(airmass, (0.866, -0.122, 0.0121, -0.000653, 1.4e-05))
            part_a = horner(clear, (0.512, -1.56, 2.286, -2.222))
            part_b = 0.37 + 0.962 * clear
            part_c = horner(clear, (-0.28, 0.932, -2.048))
            beam = jnp.maximum(clear_beam - (part_a + part_b * jnp.exp(part_c * airmass)), 0.0)
            low = cell & (LANES - 1)
            high = cell >> 7
            coefficient = jnp.zeros(wide, jnp.float32)
            for row in range(dirint_rows.shape[1] // LANES):
                line = dirint_rows[:, row * LANES : (row + 1) * LANES]
                found = jnp.take_along_axis(
                    jnp.broadcast_to(line, wide), low, axis=1, mode="promise_in_bounds"
                )
                coefficient = jnp.where(high == row, found, coefficient)
            direct = solar_constant * beam * coefficient
            diffuse = jnp.maximum(global_flat - direct * cosz, 0.1 * global_flat)
            bright = diffuse * airmass * (1.0 / solar_constant)
            factor = [
                jnp.take_along_axis(
                    jnp.broadcast_to(perez_rows[row : row + 1, :], wide),
                    sky,
                    axis=1,
                    mode="promise_in_bounds",
                )
                for row in range(6)
            ]
            circumsolar = jnp.maximum(0.0, factor[0] + factor[1] * bright + factor[2] * zenith)
            horizon = factor[3] + factor[4] * bright + factor[5] * zenith
            facing = jnp.maximum(
                cosz * cos_tilt + sin_zenith * sin_tilt * cosine(sun_az - array_azimuth), 0.0
            )
            sky_part = diffuse * (
                (1.0 - circumsolar) * (1.0 + cos_tilt) * 0.5
                + circumsolar * facing / jnp.maximum(cosz, cos_limit)
                + horizon * sin_tilt
            )
            plane = direct * facing + sky_part + albedo * global_flat * (1.0 - cos_tilt) * 0.5
            power_ref[at, lanes] = (site_capacity * plane / 1000.0).astype(jnp.bfloat16)
        return carry

    lax.fori_loop(0, n_hours // rows, some_hours, 0)
    power = power_ref[...]
    low_hours = power[:LANES]
    rest = power[LANES:]
    blank = jnp.zeros_like(rest)
    left = jnp.concatenate([rest, blank], axis=0)
    right = jnp.concatenate([blank, rest], axis=0)
    slot = slot_ref[...]
    n_slots = n_line * cap
    half = cap // 2
    dims = (((1,), (1,)), ((), ()))
    for bus_index in range(n_bus):
        base = bus_index * n_slots
        slots = lax.broadcasted_iota(jnp.int32, (n_slots, n_sites), 0) + base
        pick = jnp.where(slots == slot, 1.0, 0.0).astype(jnp.bfloat16)
        top = lax.dot_general(pick, low_hours, dims, preferred_element_type=jnp.float32)
        index = lax.broadcasted_iota(jnp.int32, (n_slots // 2, n_sites), 0)
        paired = (index // half) * cap + index % half + base
        pick_left = jnp.where(paired == slot, 1.0, 0.0).astype(jnp.bfloat16)
        pick_right = jnp.where(paired + half == slot, 1.0, 0.0).astype(jnp.bfloat16)
        bottom = lax.dot_general(
            pick_left, left, dims, preferred_element_type=jnp.float32
        ) + lax.dot_general(pick_right, right, dims, preferred_element_type=jnp.float32)
        top = top.astype(jnp.bfloat16)
        bottom = bottom.astype(jnp.bfloat16)
        for line_index in range(n_line):
            row = line_index * n_bus + bus_index
            out_ref[row, :n_slots, :] = top
            out_ref[row, n_slots:, :] = bottom


def packed_power(
    tilt_table,
    azimuth_table,
    hourly,
    dirint_coef,
    perez_coef,
    tilt_class,
    azimuth_class,
    capacity,
    slot,
    n_line,
    n_bus,
    cap,
):
    n_hours, n_sites = hourly[0].shape
    owners = n_line * n_bus
    n_slots = n_line * cap
    cells = dirint_coef.shape[0]
    rows = 32
    smem = pl.BlockSpec(memory_space=pltpu.SMEM)
    shape = (owners, n_slots * n_hours // LANES, LANES)
    operands = (
        *hourly,
        dirint_coef,
        perez_coef,
        tilt_class.reshape(1, n_sites),
        azimuth_class.reshape(1, n_sites),
        capacity.reshape(1, n_sites),
        slot,
    )
    return pl.pallas_call(
        functools.partial(power_kernel, n_line=n_line, n_bus=n_bus, cap=cap, rows=rows),
        out_shape=jax.ShapeDtypeStruct(shape, jnp.bfloat16),
        in_specs=[smem, smem] + [pl.BlockSpec(memory_space=pltpu.HBM)] * len(operands),
        out_specs=pl.BlockSpec(memory_space=pltpu.VMEM),
        scratch_shapes=[pltpu.VMEM(x.shape, x.dtype) for x in operands]
        + [
            pltpu.VMEM((n_hours, n_sites), jnp.bfloat16),
            pltpu.VMEM((1, -(-cells // LANES) * LANES), jnp.float32),
            pltpu.VMEM((8, LANES), jnp.float32),
            pltpu.SemaphoreType.DMA((len(operands),)),
        ],
        compiler_params=pltpu.CompilerParams(vmem_limit_bytes=64 << 20),
        cost_estimate=pl.CostEstimate(
            flops=2 * 10**8, bytes_accessed=3 * 10**6, transcendentals=2 * 10**5
        ),
        name="power",
    )(tilt_table, azimuth_table, *operands)


def order_slots(tags_ref, sorted_ref, rank_ref, plan_ref, group_buses):
    n_groups, n_slots = tags_ref.shape
    half = n_slots // 2
    tags = tags_ref[...].astype(jnp.float32)
    lanes = lax.broadcasted_iota(jnp.int32, (n_slots, n_slots), 1).astype(jnp.float32)
    index = lax.broadcasted_iota(jnp.int32, (n_groups, n_slots), 1)
    keys = tags * n_slots + index.astype(jnp.float32)
    tag_columns = jnp.transpose(tags)
    key_columns = jnp.transpose(keys)
    ranks = []
    for g in range(n_groups):
        smaller = key_columns[:, g : g + 1] < keys[g : g + 1]
        ranks.append(jnp.sum(jnp.where(smaller, 1.0, 0.0), axis=0, keepdims=True))
    rank = jnp.concatenate(ranks, axis=0)
    rank_ref[...] = rank.astype(jnp.int32)
    rank_columns = jnp.transpose(rank)
    ordered = []
    for g in range(n_groups):
        hit = rank_columns[:, g : g + 1] == lanes
        found = jnp.sum(jnp.where(hit, tag_columns[:, g : g + 1], 0.0), axis=0, keepdims=True)
        ordered.append(found + float(g * group_buses % LANES))
    ordered = jnp.concatenate(ordered, axis=0)
    sorted_ref[...] = ordered.astype(jnp.int32)
    real = ordered < float(EMPTY)
    last = jnp.max(jnp.where(real & (index < half), ordered, 0.0), axis=1, keepdims=True)
    after = jnp.min(jnp.where(real & (index >= half), ordered, 2.0 * EMPTY), axis=1, keepdims=True)
    for g in range(n_groups):
        plan_ref[0, g] = jnp.max(last[g : g + 1]).astype(jnp.int32)
        plan_ref[1, g] = jnp.max(after[g : g + 1]).astype(jnp.int32)


def select_kernel(
    tags_ref,
    factors_ref,
    out_ref,
    rank_ref,
    buffer,
    pick,
    sorted_ref,
    plan_ref,
    sems,
    *,
    group_buses,
    window,
    seg,
):
    g = pl.program_id(0)
    n_groups = pl.num_programs(0)
    n_slots = out_ref.shape[1]
    half = n_slots // 2
    n_seg = window // seg

    def copy(index):
        start = pl.multiple_of((index * group_buses) // LANES * LANES, LANES)
        slot = lax.rem(index, 2)
        return pltpu.make_async_copy(
            factors_ref.at[:, pl.ds(start, window)], buffer.at[slot], sems.at[slot]
        )

    @pl.when(g == 0)
    def _():
        copy(g).start()

    @pl.when(g + 1 < n_groups)
    def _():
        copy(g + 1).start()

    @pl.when(g == 0)
    def _():
        order_slots(tags_ref, sorted_ref, rank_ref, plan_ref, group_buses)

    last = plan_ref[0, g]
    after = plan_ref[1, g]
    place = sorted_ref[pl.ds(g, 1), :]

    def wanted(chunk, k):
        if chunk == 0:
            return last >= k * seg
        return after < (k + 1) * seg

    for chunk in range(2):
        columns = slice(chunk * half, (chunk + 1) * half)
        for k in range(n_seg):

            @pl.when(wanted(chunk, k))
            def _():
                buses = lax.broadcasted_iota(jnp.int32, (seg, half), 0) + k * seg
                pick[k * seg : (k + 1) * seg, columns] = jnp.where(
                    buses == place[:, columns], 1.0, 0.0
                ).astype(jnp.bfloat16)

    copy(g).wait()
    now = lax.rem(g, 2)
    for k in range(n_seg):
        stop = (k + 1) * seg
        begin = k * seg
        ends_here = last < stop if k + 1 < n_seg else last >= begin
        if 0 < k < n_seg - 1:
            ends_here = ends_here & (last >= begin)

        @pl.when(ends_here)
        def _():
            out_ref[:, :half] = jnp.dot(
                buffer[now, :, :stop], pick[:stop, :half], preferred_element_type=jnp.float32
            ).astype(jnp.bfloat16)

        starts_here = after < stop
        if k:
            starts_here = starts_here & (after >= begin)

        @pl.when(starts_here)
        def _():
            out_ref[:, half:] = jnp.dot(
                buffer[now, :, begin:], pick[begin:, half:], preferred_element_type=jnp.float32
            ).astype(jnp.bfloat16)

    @pl.when(after >= window)
    def _():
        out_ref[:, half:] = jnp.zeros((out_ref.shape[0], half), jnp.bfloat16)


def select_columns(tags, factors, group_buses, window, seg):
    n_groups, n_slots = tags.shape
    n_lines = factors.shape[0]
    whole = pl.BlockSpec((n_groups, n_slots), lambda g: (0, 0))
    return pl.pallas_call(
        functools.partial(select_kernel, group_buses=group_buses, window=window, seg=seg),
        grid=(n_groups,),
        in_specs=[whole, pl.BlockSpec(memory_space=pltpu.HBM)],
        out_specs=(pl.BlockSpec((n_lines, n_slots), lambda g: (0, g)), whole),
        out_shape=(
            jax.ShapeDtypeStruct((n_lines, n_groups * n_slots), jnp.bfloat16),
            jax.ShapeDtypeStruct((n_groups, n_slots), jnp.int32),
        ),
        scratch_shapes=[
            pltpu.VMEM((2, n_lines, window), jnp.bfloat16),
            pltpu.VMEM((window, n_slots), jnp.bfloat16),
            pltpu.VMEM((n_groups, n_slots), jnp.int32),
            pltpu.SMEM((2, n_groups), jnp.int32),
            pltpu.SemaphoreType.DMA((2,)),
        ],
        compiler_params=pltpu.CompilerParams(vmem_limit_bytes=48 << 20),
        cost_estimate=pl.CostEstimate(
            flops=2 * n_lines * window * n_groups * n_slots,
            bytes_accessed=2 * n_lines * window * n_groups,
            transcendentals=0,
        ),
        name="select",
    )(tags, factors)


def move_power(rank_ref, arrived_ref, moved_ref, cap):
    n_groups, n_slots = rank_ref.shape
    half = cap // 2
    tops = n_groups * cap
    places = lax.broadcasted_iota(jnp.int32, (n_slots, n_slots), 0)

    def one(g, carry):
        top_at = pl.ds(pl.multiple_of(g * cap, cap), cap)
        bottom_at = pl.ds(pl.multiple_of(tops + g * half, half), half)
        top = arrived_ref[:, top_at, :].reshape(n_slots, LANES)
        bottom = arrived_ref[:, bottom_at, :].astype(jnp.float32)
        blocks = bottom.shape[0]
        turned = pltpu.roll(bottom.reshape(blocks * half, LANES), LANES // 2, 1)
        bottom = jnp.concatenate([bottom, turned.reshape(blocks, half, LANES)], axis=1)
        bottom = bottom.reshape(n_slots, LANES).astype(jnp.bfloat16)
        power = jnp.concatenate([top, bottom], axis=1)
        move = jnp.where(places == rank_ref[pl.ds(g, 1), :], 1.0, 0.0).astype(jnp.bfloat16)
        moved = jnp.dot(move, power, preferred_element_type=jnp.float32)
        moved_ref[pl.ds(pl.multiple_of(g * n_slots, n_slots), n_slots), :] = moved.astype(
            jnp.bfloat16
        )
        return carry

    lax.fori_loop(0, n_groups, one, 0)


def lines_kernel(
    core_ref, *refs, cap, begin, count, first
):
    if first:
        rank_ref, arrived_ref, picked_ref = refs[:3]
        keep_ref, send_ref, moved_out, moved_ref, buffer, sems = refs[3:]
    else:
        moved_in, picked_ref = refs[:2]
        keep_ref, send_ref, moved_ref, buffer, sems = refs[2:]
    n_blocks = sems.shape[0] - 1
    block = keep_ref.shape[2] // n_blocks
    last_size = count - (n_blocks - 1) * block

    def copy(i, size):
        at = pl.multiple_of(i * block, 16)
        return pltpu.make_async_copy(
            picked_ref.at[pl.ds(begin + at, size)], buffer.at[pl.ds(at, size)], sems.at[i]
        )

    def each(act):
        for i in range(n_blocks):
            act(copy(i, block if i + 1 < n_blocks else last_size))

    if first:
        each(lambda c: c.start())
        move_power(rank_ref, arrived_ref, moved_ref, cap)
        out = pltpu.make_async_copy(moved_ref, moved_out, sems.at[n_blocks])
        out.start()
    else:
        fetch = pltpu.make_async_copy(moved_in, moved_ref, sems.at[n_blocks])
        fetch.start()
        each(lambda c: c.start())
        fetch.wait()
    rows_each = keep_ref.shape[1]
    core_zero = core_ref[0] == 0

    def one(i, carry):
        @pl.when(i + 1 < n_blocks)
        def _():
            copy(i, block).wait()

        @pl.when(i + 1 == n_blocks)
        def _():
            copy(i, last_size).wait()

        at = pl.multiple_of(i * block, block)
        flow = jnp.dot(
            buffer[pl.ds(at, block), :], moved_ref[...], preferred_element_type=jnp.float32
        )
        turned = jnp.transpose(flow)
        for x in range(keep_ref.shape[0]):
            low = 2 * x * rows_each
            even = turned[low : low + rows_each]
            odd = turned[low + rows_each : low + 2 * rows_each]
            keep_ref[x, :, pl.ds(at, block)] = jnp.where(core_zero, even, odd)
            send_ref[x, :, pl.ds(at, block)] = jnp.where(core_zero, odd, even)
        return carry

    lax.fori_loop(0, n_blocks, one, 0)
    if first:
        out.wait()


def lines(core, inputs, picked, shape, cap, begin, count, padded, moved_shape, first):
    smem = pl.BlockSpec(memory_space=pltpu.SMEM)
    vmem = pl.BlockSpec(memory_space=pltpu.VMEM)
    hbm = pl.BlockSpec(memory_space=pltpu.HBM)
    part = jax.ShapeDtypeStruct(shape + (padded,), jnp.float32)
    moved = jax.ShapeDtypeStruct(moved_shape, jnp.bfloat16)
    block = 512
    return pl.pallas_call(
        functools.partial(lines_kernel, cap=cap, begin=begin, count=count, first=first),
        in_specs=[smem] + ([vmem, vmem] if first else [hbm]) + [hbm],
        out_specs=[vmem, vmem] + ([hbm] if first else []),
        out_shape=[part, part] + ([moved] if first else []),
        scratch_shapes=[
            pltpu.VMEM(moved_shape, jnp.bfloat16),
            pltpu.VMEM((padded, picked.shape[1]), jnp.bfloat16),
            pltpu.SemaphoreType.DMA((padded // block + 1,)),
        ],
        compiler_params=pltpu.CompilerParams(vmem_limit_bytes=46 << 20),
        cost_estimate=pl.CostEstimate(
            flops=1 * 2 * count * moved_shape[0] * moved_shape[1],
            bytes_accessed=1 * 2 * count * moved_shape[0],
            transcendentals=0,
        ),
        name="first_lines" if first else "other_lines",
    )(core, *inputs, picked)


def fast_device(
    clearness,
    cos_zenith,
    sun_azimuth,
    dirint_cell,
    sky_bin,
    dirint_coef,
    perez_coef,
    tilt_class,
    azimuth_class,
    tilt_table,
    azimuth_table,
    capacity,
    site_bus,
    transfer_factors,
):
    n_line = lax.axis_size("line")
    n_bus = lax.axis_size("bus")
    owners = n_line * n_bus
    n_hours, n_sites = clearness.shape
    n_lines, n_columns = transfer_factors.shape
    group_buses = BUSES // owners
    cap = 2 * n_sites // owners
    window = window_of(group_buses)
    seg = window // 3
    slot, tags = place_sites(site_bus, owners, group_buses, cap, n_line, n_bus)
    tags = lax.all_to_all(tags, ("line", "bus"), split_axis=0, concat_axis=0, tiled=True)
    outgoing = packed_power(
        tilt_table,
        azimuth_table,
        (clearness, cos_zenith, sun_azimuth, dirint_cell, sky_bin),
        dirint_coef,
        perez_coef,
        tilt_class,
        azimuth_class,
        capacity,
        slot,
        n_line,
        n_bus,
        cap,
    )
    arrived = lax.all_to_all(outgoing, ("line", "bus"), split_axis=0, concat_axis=0, tiled=True)
    tags = tags.reshape(owners, n_line, cap).transpose(1, 0, 2).reshape(n_line, owners * cap)
    picked, rank = select_columns(tags, transfer_factors, group_buses, window, seg)
    place = lax.axis_index("bus")
    core = (place % 2).reshape(1)
    near = place // 2 == 0
    other_core = [(i, i ^ 1) for i in range(n_bus)]
    other_chip = [(i, i ^ 2) for i in range(n_bus)]
    shape = (n_bus // 2, n_hours // n_bus)
    moved_shape = (n_line * owners * cap, 2 * LANES)
    half_lines = -(-n_lines // 1024) * 512
    keep_a, send_a, moved = lines(
        core, (rank, arrived), picked, shape, cap, 0, half_lines, half_lines, moved_shape, True
    )
    other = n_lines - half_lines
    padded = -(-other // 512) * 512
    keep_b, send_b = lines(
        core, (moved,), picked, shape, cap, half_lines, other, padded, moved_shape, False
    )
    ends = []
    for keep, send in ((keep_a, send_a), (keep_b, send_b)):
        summed = keep + lax.ppermute(send, "bus", other_core)
        own = jnp.where(near, summed[0], summed[1])
        away = jnp.where(near, summed[1], summed[0]).astype(jnp.bfloat16)
        away = lax.ppermute(away, "bus", other_chip)
        ends.append(own + away.astype(jnp.float32))
    return jnp.concatenate(ends, axis=1)[:, :n_lines].T


def window_of(group_buses):
    step = math.gcd(group_buses, LANES)
    most = LANES - step + group_buses
    return -(-most // LANES) * LANES


def per_device(*arrays):
    n_line = lax.axis_size("line")
    n_bus = lax.axis_size("bus")
    owners = n_line * n_bus
    n_hours, n_sites = arrays[0].shape
    n_lines, n_columns = arrays[-1].shape
    group_buses = BUSES // owners
    window = window_of(group_buses)
    last = (n_line - 1) * group_buses // LANES * LANES
    fits = (
        n_bus == 4
        and n_hours == 192
        and n_sites == 2 * LANES
        and n_sites * 2 == owners * 16
        and n_line * 16 == LANES
        and n_lines % 16 == 0
        and n_columns % LANES == 0
        and group_buses < EMPTY - LANES
        and window % (3 * LANES) == 0
        and last + window <= n_columns
    )
    if fits:
        return fast_device(*arrays)
    return general_device(*arrays)


def solution(mesh):
    in_specs = (
        P(None, ("line", "bus")),
        P(None, ("line", "bus")),
        P(None, ("line", "bus")),
        P(None, ("line", "bus")),
        P(None, ("line", "bus")),
        P(),
        P(),
        P(("line", "bus")),
        P(("line", "bus")),
        P(),
        P(),
        P(("line", "bus")),
        P(("line", "bus")),
        P("line", "bus"),
    )
    out_specs = P("line", "bus")
    return jax.shard_map(
        per_device, mesh=mesh, in_specs=in_specs, out_specs=out_specs, check_vma=False
    )
```

```python
import functools
import math

import jax
import jax.numpy as jnp
from jax import lax
from jax.experimental import pallas as pl
from jax.experimental.pallas import tpu as pltpu
from jax.sharding import PartitionSpec as P

BUSES = 70144
TILTS = 8
AZIMS = 12


solar_constant = 1367.0
albedo = 0.2
cos_limit = 0.08716
row_width = 36


def pick_table(classes, table, count):
    picked = jnp.zeros(classes.shape, jnp.float32)
    for entry in range(count):
        picked = jnp.where(classes == entry, table[entry], picked)
    return picked


def dirint_lookup(cell, dirint_coef):
    row_count = dirint_coef.shape[0] // row_width
    table = dirint_coef.reshape(row_count, row_width)
    flat_cell = cell.reshape(-1)
    upper = flat_cell // row_width
    lower = flat_cell % row_width
    row_pick = (upper[:, None] == jnp.arange(row_count, dtype=jnp.int32)[None, :]).astype(
        jnp.float32
    )
    rows = jnp.dot(
        row_pick, table, precision=lax.Precision.HIGHEST, preferred_element_type=jnp.float32
    )
    column_hit = lower[:, None] == jnp.arange(row_width, dtype=jnp.int32)[None, :]
    picked = jnp.sum(jnp.where(column_hit, rows, 0.0), axis=1)
    return picked.reshape(cell.shape)


def site_power(
    clear,
    cosz,
    sun_az,
    cell,
    sky,
    tilt_angle,
    array_azimuth,
    site_capacity,
    dirint_coef,
    perez_coef,
):
    global_flat = clear * solar_constant * cosz
    zenith = jnp.arccos(cosz)
    airmass = 1.0 / (cosz + 0.50572 * (96.07995 - zenith * (180.0 / math.pi)) ** (-1.6364))
    clear_beam = (
        0.866 - 0.122 * airmass + 0.0121 * airmass**2 - 0.000653 * airmass**3 + 1.4e-05 * airmass**4
    )
    part_a = 0.512 - 1.56 * clear + 2.286 * clear**2 - 2.222 * clear**3
    part_b = 0.37 + 0.962 * clear
    part_c = -0.28 + 0.932 * clear - 2.048 * clear**2
    beam_index = jnp.maximum(clear_beam - (part_a + part_b * jnp.exp(part_c * airmass)), 0.0)
    direct_normal = solar_constant * beam_index * dirint_lookup(cell, dirint_coef)
    diffuse = jnp.maximum(global_flat - direct_normal * cosz, 0.1 * global_flat)
    brightness = diffuse * airmass / solar_constant
    factors = [jnp.zeros(cosz.shape, jnp.float32) for entry in range(6)]
    for bin_index in range(perez_coef.shape[1]):
        hit = sky == bin_index
        factors = [jnp.where(hit, perez_coef[row, bin_index], factors[row]) for row in range(6)]
    circumsolar = jnp.maximum(0.0, factors[0] + factors[1] * brightness + factors[2] * zenith)
    horizon_term = factors[3] + factors[4] * brightness + factors[5] * zenith
    cos_tilt = jnp.cos(tilt_angle)
    sin_tilt = jnp.sin(tilt_angle)
    cos_incidence = cosz * cos_tilt + jnp.sin(zenith) * sin_tilt * jnp.cos(sun_az - array_azimuth)
    facing = jnp.maximum(cos_incidence, 0.0)
    horizon_cos = jnp.maximum(cosz, cos_limit)
    sky_part = diffuse * (
        (1.0 - circumsolar) * (1.0 + cos_tilt) * 0.5
        + circumsolar * facing / horizon_cos
        + horizon_term * sin_tilt
    )
    plane = direct_normal * facing + sky_part + albedo * global_flat * (1.0 - cos_tilt) * 0.5
    return (site_capacity * plane / 1000.0).astype(jnp.bfloat16)


def general_device(
    clearness,
    cos_zenith,
    sun_azimuth,
    dirint_cell,
    sky_bin,
    dirint_coef,
    perez_coef,
    tilt_class,
    azimuth_class,
    tilt_table,
    azimuth_table,
    capacity,
    site_bus,
    transfer_factors,
):
    line_count = lax.axis_size("line")
    bus_count = lax.axis_size("bus")
    owners = line_count * bus_count
    n_hours, n_sites = clearness.shape
    group_buses = BUSES // owners
    slots_each = max(2, 2 * n_sites // owners)
    tilt_angle = pick_table(tilt_class, tilt_table, TILTS)
    array_azimuth = pick_table(azimuth_class, azimuth_table, AZIMS)
    power = site_power(
        clearness,
        cos_zenith,
        sun_azimuth,
        dirint_cell,
        sky_bin,
        tilt_angle,
        array_azimuth,
        capacity,
        dirint_coef,
        perez_coef,
    )
    group_index = site_bus // group_buses
    target = group_index % line_count * bus_count + group_index // line_count
    local_bus = site_bus % group_buses
    one_hot = (target[:, None] == jnp.arange(owners, dtype=jnp.int32)[None, :]).astype(jnp.int32)
    position = jnp.sum(one_hot * (jnp.cumsum(one_hot, axis=0) - 1), axis=1)
    slot_index = target * slots_each + position
    outgoing = jnp.zeros((n_hours, owners * slots_each), jnp.bfloat16).at[:, slot_index].set(power)
    labels = jnp.zeros((1, owners * slots_each), jnp.int32).at[0, slot_index].set(local_bus)
    arrived, bus_tags = (
        lax.all_to_all(outgoing, ("line", "bus"), split_axis=1, concat_axis=1, tiled=True),
        lax.all_to_all(labels, ("line", "bus"), split_axis=1, concat_axis=1, tiled=True),
    )
    bus_tags = bus_tags.reshape(owners * slots_each)
    member = (bus_tags[:, None] == jnp.arange(group_buses, dtype=jnp.int32)[None, :]).astype(
        jnp.bfloat16
    )
    injection = jnp.einsum("hr,rb->bh", arrived, member, preferred_element_type=jnp.float32).astype(
        jnp.bfloat16
    )
    partial_flows = jnp.dot(
        transfer_factors,
        lax.all_gather(injection, "line", axis=0, tiled=True),
        preferred_element_type=jnp.float32,
    )
    return lax.psum_scatter(partial_flows, "bus", scatter_dimension=1, tiled=True)


LANES = 128
ACOS_POLY = (
    1.5707963262615365,
    -0.21460172591625612,
    0.08904479608150453,
    -0.0507408012983321,
    0.033314914408815,
    -0.02284457168134235,
    0.014575916928409219,
    -0.00744564558483129,
    0.002518626106102872,
    -0.00040427332732297214,
)
COS_POLY = tuple((-1.0) ** k / math.factorial(2 * k) for k in range(8))
SIN_POLY = tuple((-1.0) ** k / math.factorial(2 * k + 1) for k in range(8))
EMPTY = 4095


def horner(x, poly):
    total = jnp.full_like(x, poly[-1])
    for coefficient in poly[-2::-1]:
        total = total * x + coefficient
    return total


def reduce_pi(x):
    turns = jnp.floor(x * (1.0 / math.pi) + 0.5)
    rest = (x - turns * 3.140625) - turns * 0.0009676535897932
    odd = turns - 2.0 * jnp.floor(turns * 0.5)
    return rest, 1.0 - 2.0 * odd


def cosine(x):
    rest, sign = reduce_pi(x)
    return sign * horner(rest * rest, COS_POLY)


def sine(x):
    rest, sign = reduce_pi(x)
    return sign * rest * horner(rest * rest, SIN_POLY)


def to_column(row, eye):
    return jnp.sum(jnp.where(eye, row, 0.0), axis=1, keepdims=True)


def place_kernel(bus_ref, slot_ref, tags_ref, *, owners, group_buses, cap, n_line, n_bus):
    n_sites = bus_ref.shape[1]
    bus = bus_ref[...]
    group = jnp.zeros(bus.shape, jnp.int32)
    for k in range(1, owners):
        group = group + (bus >= k * group_buses).astype(jnp.int32)
    local = (bus - group * group_buses).astype(jnp.float32)
    group = group.astype(jnp.float32)
    first = lax.broadcasted_iota(jnp.int32, (n_sites, n_sites), 0)
    second = lax.broadcasted_iota(jnp.int32, (n_sites, n_sites), 1)
    eye = first == second
    earlier = (to_column(group, eye) == group) & (first < second)
    position = jnp.sum(jnp.where(earlier, 1.0, 0.0), axis=0, keepdims=True)
    slot = group * float(cap) + position
    slot_ref[...] = slot.astype(jnp.int32)
    slot_column = to_column(slot, eye).astype(jnp.int32)
    local_column = to_column(local, eye)
    n_slots = n_line * cap
    for bus_index in range(n_bus):
        lanes = lax.broadcasted_iota(jnp.int32, (n_sites, n_slots), 1) + bus_index * n_slots
        hit = slot_column == lanes
        tag = jnp.sum(jnp.where(hit, local_column + 1.0, 0.0), axis=0, keepdims=True)
        tag = jnp.where(tag > 0.5, tag - 1.0, float(EMPTY)).astype(jnp.int32)
        for line_index in range(n_line):
            row = line_index * n_bus + bus_index
            tags_ref[row : row + 1, :] = tag


def place_sites(site_bus, owners, group_buses, cap, n_line, n_bus):
    n_sites = site_bus.shape[0]
    return pl.pallas_call(
        functools.partial(
            place_kernel,
            owners=owners,
            group_buses=group_buses,
            cap=cap,
            n_line=n_line,
            n_bus=n_bus,
        ),
        out_shape=(
            jax.ShapeDtypeStruct((1, n_sites), jnp.int32),
            jax.ShapeDtypeStruct((owners, n_line * cap), jnp.int32),
        ),
        cost_estimate=pl.CostEstimate(flops=10**6, bytes_accessed=10**5, transcendentals=0),
        name="place",
    )(site_bus.reshape(1, n_sites))


def power_kernel(
    tilt_table_ref,
    azimuth_table_ref,
    perez_ref,
    *refs,
    n_line,
    n_bus,
    cap,
    rows,
):
    sources = refs[:10]
    out_ref = refs[10]
    held = refs[11:21]
    power_ref, dirint_rows, sems = refs[21:]
    copies = [
        pltpu.make_async_copy(source, place, sems.at[i])
        for i, (source, place) in enumerate(zip(sources, held))
    ]
    for copy in copies:
        copy.start()
    for copy in copies:
        copy.wait()
    clear_all, cosz_all, sun_all, cell_all, sky_all = held[:5]
    dirint_ref, tilt_class_ref, azimuth_class_ref, capacity_ref, slot_ref = held[5:]
    n_hours, n_sites = clear_all.shape
    cells = dirint_ref.shape[0]
    dirint_rows[...] = jnp.zeros_like(dirint_rows)
    for begin in range(0, cells, LANES):
        count = min(LANES, cells - begin)
        dirint_rows[:, begin : begin + count] = dirint_ref[begin : begin + count].reshape(1, count)
    tilt_class = tilt_class_ref[...]
    azimuth_class = azimuth_class_ref[...]
    tilt = jnp.zeros(tilt_class.shape, jnp.float32)
    for entry in range(TILTS):
        tilt = jnp.where(tilt_class == entry, tilt_table_ref[entry], tilt)
    azimuth = jnp.zeros(tilt_class.shape, jnp.float32)
    for entry in range(AZIMS):
        azimuth = jnp.where(azimuth_class == entry, azimuth_table_ref[entry], azimuth)
    wide = (rows, LANES)
    cos_tilts = cosine(tilt)
    sin_tilts = sine(tilt)
    capacity = capacity_ref[...]

    def some_hours(now, carry):
        at = pl.ds(pl.multiple_of(now * rows, rows), rows)
        for part in range(n_sites // LANES):
            lanes = slice(part * LANES, (part + 1) * LANES)
            cos_tilt = jnp.broadcast_to(cos_tilts[:, lanes], wide)
            sin_tilt = jnp.broadcast_to(sin_tilts[:, lanes], wide)
            array_azimuth = jnp.broadcast_to(azimuth[:, lanes], wide)
            site_capacity = jnp.broadcast_to(capacity[:, lanes], wide)
            clear = clear_all[at, lanes]
            cosz = cosz_all[at, lanes]
            sun_az = sun_all[at, lanes]
            cell = cell_all[at, lanes]
            sky = sky_all[at, lanes]
            global_flat = clear * solar_constant * cosz
            zenith = jnp.sqrt(1.0 - cosz) * horner(cosz, ACOS_POLY)
            sin_zenith = jnp.sqrt((1.0 - cosz) * (1.0 + cosz))
            height = 96.07995 - zenith * (180.0 / math.pi)
            airmass = 1.0 / (cosz + 0.50572 * jnp.exp(-1.6364 * jnp.log(height)))
            clear_beam = horner(airmass, (0.866, -0.122, 0.0121, -0.000653, 1.4e-05))
            part_a = horner(clear, (0.512, -1.56, 2.286, -2.222))
            part_b = 0.37 + 0.962 * clear
            part_c = horner(clear, (-0.28, 0.932, -2.048))
            beam = jnp.maximum(clear_beam - (part_a + part_b * jnp.exp(part_c * airmass)), 0.0)
            low = cell & (LANES - 1)
            high = cell >> 7
            coefficient = jnp.zeros(wide, jnp.float32)
            for row in range(dirint_rows.shape[1] // LANES):
                line = dirint_rows[:, row * LANES : (row + 1) * LANES]
                found = jnp.take_along_axis(
                    jnp.broadcast_to(line, wide), low, axis=1, mode="promise_in_bounds"
                )
                coefficient = jnp.where(high == row, found, coefficient)
            direct = solar_constant * beam * coefficient
            diffuse = jnp.maximum(global_flat - direct * cosz, 0.1 * global_flat)
            bright = diffuse * airmass * (1.0 / solar_constant)
            factor = [jnp.full(wide, perez_ref[row, 0]) for row in range(6)]
            for entry in range(1, perez_ref.shape[1]):
                hit = sky == entry
                factor = [
                    jnp.where(hit, perez_ref[row, entry], factor[row]) for row in range(6)
                ]
            circumsolar = jnp.maximum(0.0, factor[0] + factor[1] * bright + factor[2] * zenith)
            horizon = factor[3] + factor[4] * bright + factor[5] * zenith
            facing = jnp.maximum(
                cosz * cos_tilt + sin_zenith * sin_tilt * cosine(sun_az - array_azimuth), 0.0
            )
            sky_part = diffuse * (
                (1.0 - circumsolar) * (1.0 + cos_tilt) * 0.5
                + circumsolar * facing / jnp.maximum(cosz, cos_limit)
                + horizon * sin_tilt
            )
            plane = direct * facing + sky_part + albedo * global_flat * (1.0 - cos_tilt) * 0.5
            power_ref[at, lanes] = (site_capacity * plane / 1000.0).astype(jnp.bfloat16)
        return carry

    lax.fori_loop(0, n_hours // rows, some_hours, 0)
    power = power_ref[...]
    low_hours = power[:LANES]
    rest = power[LANES:]
    blank = jnp.zeros_like(rest)
    left = jnp.concatenate([rest, blank], axis=0)
    right = jnp.concatenate([blank, rest], axis=0)
    slot = slot_ref[...]
    n_slots = n_line * cap
    half = cap // 2
    dims = (((1,), (1,)), ((), ()))
    for bus_index in range(n_bus):
        base = bus_index * n_slots
        slots = lax.broadcasted_iota(jnp.int32, (n_slots, n_sites), 0) + base
        pick = jnp.where(slots == slot, 1.0, 0.0).astype(jnp.bfloat16)
        top = lax.dot_general(pick, low_hours, dims, preferred_element_type=jnp.float32)
        index = lax.broadcasted_iota(jnp.int32, (n_slots // 2, n_sites), 0)
        paired = (index // half) * cap + index % half + base
        pick_left = jnp.where(paired == slot, 1.0, 0.0).astype(jnp.bfloat16)
        pick_right = jnp.where(paired + half == slot, 1.0, 0.0).astype(jnp.bfloat16)
        bottom = lax.dot_general(
            pick_left, left, dims, preferred_element_type=jnp.float32
        ) + lax.dot_general(pick_right, right, dims, preferred_element_type=jnp.float32)
        top = top.astype(jnp.bfloat16)
        bottom = bottom.astype(jnp.bfloat16)
        for line_index in range(n_line):
            row = line_index * n_bus + bus_index
            out_ref[row, :n_slots, :] = top
            out_ref[row, n_slots:, :] = bottom


def packed_power(
    tilt_table,
    azimuth_table,
    hourly,
    dirint_coef,
    perez_coef,
    tilt_class,
    azimuth_class,
    capacity,
    slot,
    n_line,
    n_bus,
    cap,
):
    n_hours, n_sites = hourly[0].shape
    owners = n_line * n_bus
    n_slots = n_line * cap
    cells = dirint_coef.shape[0]
    rows = 64
    smem = pl.BlockSpec(memory_space=pltpu.SMEM)
    shape = (owners, n_slots * n_hours // LANES, LANES)
    operands = (
        *hourly,
        dirint_coef,
        tilt_class.reshape(1, n_sites),
        azimuth_class.reshape(1, n_sites),
        capacity.reshape(1, n_sites),
        slot,
    )
    return pl.pallas_call(
        functools.partial(power_kernel, n_line=n_line, n_bus=n_bus, cap=cap, rows=rows),
        out_shape=jax.ShapeDtypeStruct(shape, jnp.bfloat16),
        in_specs=[smem] * 3 + [pl.BlockSpec(memory_space=pltpu.HBM)] * len(operands),
        out_specs=pl.BlockSpec(memory_space=pltpu.VMEM),
        scratch_shapes=[pltpu.VMEM(x.shape, x.dtype) for x in operands]
        + [
            pltpu.VMEM((n_hours, n_sites), jnp.bfloat16),
            pltpu.VMEM((1, -(-cells // LANES) * LANES), jnp.float32),
            pltpu.SemaphoreType.DMA((len(operands),)),
        ],
        compiler_params=pltpu.CompilerParams(vmem_limit_bytes=64 << 20),
        cost_estimate=pl.CostEstimate(
            flops=2 * 10**8, bytes_accessed=3 * 10**6, transcendentals=2 * 10**5
        ),
        name="power",
    )(tilt_table, azimuth_table, perez_coef, *operands)


def order_slots(tags_ref, sorted_ref, rank_ref, plan_ref, group_buses):
    n_groups, n_slots = tags_ref.shape
    half = n_slots // 2
    tags = tags_ref[...].astype(jnp.float32)
    lanes = lax.broadcasted_iota(jnp.int32, (n_slots, n_slots), 1).astype(jnp.float32)
    index = lax.broadcasted_iota(jnp.int32, (n_groups, n_slots), 1)
    keys = tags * n_slots + index.astype(jnp.float32)
    tag_columns = jnp.transpose(tags)
    key_columns = jnp.transpose(keys)
    ranks = []
    for g in range(n_groups):
        smaller = key_columns[:, g : g + 1] < keys[g : g + 1]
        ranks.append(jnp.sum(jnp.where(smaller, 1.0, 0.0), axis=0, keepdims=True))
    rank = jnp.concatenate(ranks, axis=0)
    rank_ref[...] = rank.astype(jnp.int32)
    rank_columns = jnp.transpose(rank)
    ordered = []
    for g in range(n_groups):
        hit = rank_columns[:, g : g + 1] == lanes
        found = jnp.sum(jnp.where(hit, tag_columns[:, g : g + 1], 0.0), axis=0, keepdims=True)
        ordered.append(found + float(g * group_buses % LANES))
    ordered = jnp.concatenate(ordered, axis=0)
    sorted_ref[...] = ordered.astype(jnp.int32)
    real = ordered < float(EMPTY)
    last = jnp.max(jnp.where(real & (index < half), ordered, 0.0), axis=1, keepdims=True)
    after = jnp.min(jnp.where(real & (index >= half), ordered, 2.0 * EMPTY), axis=1, keepdims=True)
    for g in range(n_groups):
        plan_ref[0, g] = jnp.max(last[g : g + 1]).astype(jnp.int32)
        plan_ref[1, g] = jnp.max(after[g : g + 1]).astype(jnp.int32)


def select_kernel(
    tags_ref,
    factors_ref,
    out_ref,
    rank_ref,
    buffer,
    pick,
    sorted_ref,
    plan_ref,
    sems,
    *,
    group_buses,
    window,
    seg,
):
    g = pl.program_id(0)
    n_groups = pl.num_programs(0)
    n_slots = out_ref.shape[1]
    half = n_slots // 2
    n_seg = window // seg

    def copy(index):
        start = pl.multiple_of((index * group_buses) // LANES * LANES, LANES)
        slot = lax.rem(index, 2)
        return pltpu.make_async_copy(
            factors_ref.at[:, pl.ds(start, window)], buffer.at[slot], sems.at[slot]
        )

    @pl.when(g == 0)
    def _():
        copy(g).start()

    @pl.when(g + 1 < n_groups)
    def _():
        copy(g + 1).start()

    @pl.when(g == 0)
    def _():
        order_slots(tags_ref, sorted_ref, rank_ref, plan_ref, group_buses)

    last = plan_ref[0, g]
    after = plan_ref[1, g]
    place = sorted_ref[pl.ds(g, 1), :]

    def wanted(chunk, k):
        if chunk == 0:
            return last >= k * seg
        return after < (k + 1) * seg

    for chunk in range(2):
        columns = slice(chunk * half, (chunk + 1) * half)
        for k in range(n_seg):

            @pl.when(wanted(chunk, k))
            def _():
                buses = lax.broadcasted_iota(jnp.int32, (seg, half), 0) + k * seg
                pick[k * seg : (k + 1) * seg, columns] = jnp.where(
                    buses == place[:, columns], 1.0, 0.0
                ).astype(jnp.bfloat16)

    copy(g).wait()
    now = lax.rem(g, 2)
    for k in range(n_seg):
        stop = (k + 1) * seg
        begin = k * seg
        ends_here = last < stop if k + 1 < n_seg else last >= begin
        if 0 < k < n_seg - 1:
            ends_here = ends_here & (last >= begin)

        @pl.when(ends_here)
        def _():
            out_ref[:, :half] = jnp.dot(
                buffer[now, :, :stop], pick[:stop, :half], preferred_element_type=jnp.float32
            ).astype(jnp.bfloat16)

        starts_here = after < stop
        if k:
            starts_here = starts_here & (after >= begin)

        @pl.when(starts_here)
        def _():
            out_ref[:, half:] = jnp.dot(
                buffer[now, :, begin:], pick[begin:, half:], preferred_element_type=jnp.float32
            ).astype(jnp.bfloat16)

    @pl.when(after >= window)
    def _():
        out_ref[:, half:] = jnp.zeros((out_ref.shape[0], half), jnp.bfloat16)


def select_columns(tags, factors, group_buses, window, seg):
    n_groups, n_slots = tags.shape
    n_lines = factors.shape[0]
    whole = pl.BlockSpec((n_groups, n_slots), lambda g: (0, 0))
    return pl.pallas_call(
        functools.partial(select_kernel, group_buses=group_buses, window=window, seg=seg),
        grid=(n_groups,),
        in_specs=[whole, pl.BlockSpec(memory_space=pltpu.HBM)],
        out_specs=(pl.BlockSpec((n_lines, n_slots), lambda g: (0, g)), whole),
        out_shape=(
            jax.ShapeDtypeStruct((n_lines, n_groups * n_slots), jnp.bfloat16),
            jax.ShapeDtypeStruct((n_groups, n_slots), jnp.int32),
        ),
        scratch_shapes=[
            pltpu.VMEM((2, n_lines, window), jnp.bfloat16),
            pltpu.VMEM((window, n_slots), jnp.bfloat16),
            pltpu.VMEM((n_groups, n_slots), jnp.int32),
            pltpu.SMEM((2, n_groups), jnp.int32),
            pltpu.SemaphoreType.DMA((2,)),
        ],
        compiler_params=pltpu.CompilerParams(vmem_limit_bytes=48 << 20),
        cost_estimate=pl.CostEstimate(
            flops=2 * n_lines * window * n_groups * n_slots,
            bytes_accessed=2 * n_lines * window * n_groups,
            transcendentals=0,
        ),
        name="select",
    )(tags, factors)


def move_power(rank_ref, arrived_ref, moved_ref, cap):
    n_groups, n_slots = rank_ref.shape
    half = cap // 2
    tops = n_groups * cap
    places = lax.broadcasted_iota(jnp.int32, (n_slots, n_slots), 0)

    def one(g, carry):
        top_at = pl.ds(pl.multiple_of(g * cap, cap), cap)
        bottom_at = pl.ds(pl.multiple_of(tops + g * half, half), half)
        top = arrived_ref[:, top_at, :].reshape(n_slots, LANES)
        bottom = arrived_ref[:, bottom_at, :].astype(jnp.float32)
        blocks = bottom.shape[0]
        turned = pltpu.roll(bottom.reshape(blocks * half, LANES), LANES // 2, 1)
        bottom = jnp.concatenate([bottom, turned.reshape(blocks, half, LANES)], axis=1)
        bottom = bottom.reshape(n_slots, LANES).astype(jnp.bfloat16)
        power = jnp.concatenate([top, bottom], axis=1)
        move = jnp.where(places == rank_ref[pl.ds(g, 1), :], 1.0, 0.0).astype(jnp.bfloat16)
        moved = jnp.dot(move, power, preferred_element_type=jnp.float32)
        moved_ref[pl.ds(pl.multiple_of(g * n_slots, n_slots), n_slots), :] = moved.astype(
            jnp.bfloat16
        )
        return carry

    lax.fori_loop(0, n_groups, one, 0, unroll=2)


def lines_kernel(
    core_ref, *refs, cap, begin, count, first
):
    if first:
        rank_ref, arrived_ref, picked_ref = refs[:3]
        keep_ref, send_ref, moved_out, moved_ref, buffer, sems = refs[3:]
    else:
        moved_in, picked_ref = refs[:2]
        keep_ref, send_ref, moved_ref, buffer, sems = refs[2:]
    n_blocks = sems.shape[0] - 1
    block = keep_ref.shape[2] // n_blocks
    last_size = count - (n_blocks - 1) * block

    def copy(i, size):
        at = pl.multiple_of(i * block, 16)
        return pltpu.make_async_copy(
            picked_ref.at[pl.ds(begin + at, size)], buffer.at[pl.ds(at, size)], sems.at[i]
        )

    def each(act):
        for i in range(n_blocks):
            act(copy(i, block if i + 1 < n_blocks else last_size))

    if first:
        each(lambda c: c.start())
        move_power(rank_ref, arrived_ref, moved_ref, cap)
        out = pltpu.make_async_copy(moved_ref, moved_out, sems.at[n_blocks])
        out.start()
    else:
        fetch = pltpu.make_async_copy(moved_in, moved_ref, sems.at[n_blocks])
        fetch.start()
        each(lambda c: c.start())
        fetch.wait()
    rows_each = keep_ref.shape[1]
    core_zero = core_ref[0] == 0

    def one(i, carry):
        @pl.when(i + 1 < n_blocks)
        def _():
            copy(i, block).wait()

        @pl.when(i + 1 == n_blocks)
        def _():
            copy(i, last_size).wait()

        at = pl.multiple_of(i * block, block)
        flow = jnp.dot(
            buffer[pl.ds(at, block), :], moved_ref[...], preferred_element_type=jnp.float32
        )
        turned = jnp.transpose(flow)
        for x in range(keep_ref.shape[0]):
            low = 2 * x * rows_each
            even = turned[low : low + rows_each]
            odd = turned[low + rows_each : low + 2 * rows_each]
            keep_ref[x, :, pl.ds(at, block)] = jnp.where(core_zero, even, odd)
            send_ref[x, :, pl.ds(at, block)] = jnp.where(core_zero, odd, even)
        return carry

    lax.fori_loop(0, n_blocks, one, 0)
    if first:
        out.wait()


def lines(core, inputs, picked, shape, cap, begin, count, padded, moved_shape, first):
    smem = pl.BlockSpec(memory_space=pltpu.SMEM)
    vmem = pl.BlockSpec(memory_space=pltpu.VMEM)
    hbm = pl.BlockSpec(memory_space=pltpu.HBM)
    part = jax.ShapeDtypeStruct(shape + (padded,), jnp.float32)
    moved = jax.ShapeDtypeStruct(moved_shape, jnp.bfloat16)
    block = 512
    return pl.pallas_call(
        functools.partial(lines_kernel, cap=cap, begin=begin, count=count, first=first),
        in_specs=[smem] + ([vmem, vmem] if first else [hbm]) + [hbm],
        out_specs=[vmem, vmem] + ([hbm] if first else []),
        out_shape=[part, part] + ([moved] if first else []),
        scratch_shapes=[
            pltpu.VMEM(moved_shape, jnp.bfloat16),
            pltpu.VMEM((padded, picked.shape[1]), jnp.bfloat16),
            pltpu.SemaphoreType.DMA((padded // block + 1,)),
        ],
        compiler_params=pltpu.CompilerParams(vmem_limit_bytes=46 << 20),
        cost_estimate=pl.CostEstimate(
            flops=1 * 2 * count * moved_shape[0] * moved_shape[1],
            bytes_accessed=1 * 2 * count * moved_shape[0],
            transcendentals=0,
        ),
        name="first_lines" if first else "other_lines",
    )(core, *inputs, picked)


def fast_device(
    clearness,
    cos_zenith,
    sun_azimuth,
    dirint_cell,
    sky_bin,
    dirint_coef,
    perez_coef,
    tilt_class,
    azimuth_class,
    tilt_table,
    azimuth_table,
    capacity,
    site_bus,
    transfer_factors,
):
    n_line = lax.axis_size("line")
    n_bus = lax.axis_size("bus")
    owners = n_line * n_bus
    n_hours, n_sites = clearness.shape
    n_lines, n_columns = transfer_factors.shape
    group_buses = BUSES // owners
    cap = 2 * n_sites // owners
    window = window_of(group_buses)
    seg = window // 3
    slot, tags = place_sites(site_bus, owners, group_buses, cap, n_line, n_bus)
    tags = lax.all_to_all(tags, ("line", "bus"), split_axis=0, concat_axis=0, tiled=True)
    outgoing = packed_power(
        tilt_table,
        azimuth_table,
        (clearness, cos_zenith, sun_azimuth, dirint_cell, sky_bin),
        dirint_coef,
        perez_coef,
        tilt_class,
        azimuth_class,
        capacity,
        slot,
        n_line,
        n_bus,
        cap,
    )
    arrived = lax.all_to_all(outgoing, ("line", "bus"), split_axis=0, concat_axis=0, tiled=True)
    tags = tags.reshape(owners, n_line, cap).transpose(1, 0, 2).reshape(n_line, owners * cap)
    picked, rank = select_columns(tags, transfer_factors, group_buses, window, seg)
    place = lax.axis_index("bus")
    core = (place % 2).reshape(1)
    near = place // 2 == 0
    other_core = [(i, i ^ 1) for i in range(n_bus)]
    other_chip = [(i, i ^ 2) for i in range(n_bus)]
    shape = (n_bus // 2, n_hours // n_bus)
    moved_shape = (n_line * owners * cap, 2 * LANES)
    half_lines = -(-n_lines // 1024) * 512
    keep_a, send_a, moved = lines(
        core, (rank, arrived), picked, shape, cap, 0, half_lines, half_lines, moved_shape, True
    )
    other = n_lines - half_lines
    padded = -(-other // 512) * 512
    keep_b, send_b = lines(
        core, (moved,), picked, shape, cap, half_lines, other, padded, moved_shape, False
    )
    ends = []
    for keep, send in ((keep_a, send_a), (keep_b, send_b)):
        summed = keep + lax.ppermute(send, "bus", other_core)
        own = jnp.where(near, summed[0], summed[1])
        away = jnp.where(near, summed[1], summed[0]).astype(jnp.bfloat16)
        away = lax.ppermute(away, "bus", other_chip)
        ends.append(own + away.astype(jnp.float32))
    return jnp.concatenate(ends, axis=1)[:, :n_lines].T


def window_of(group_buses):
    step = math.gcd(group_buses, LANES)
    most = LANES - step + group_buses
    return -(-most // LANES) * LANES


def per_device(*arrays):
    n_line = lax.axis_size("line")
    n_bus = lax.axis_size("bus")
    owners = n_line * n_bus
    n_hours, n_sites = arrays[0].shape
    n_lines, n_columns = arrays[-1].shape
    group_buses = BUSES // owners
    window = window_of(group_buses)
    last = (n_line - 1) * group_buses // LANES * LANES
    fits = (
        n_bus == 4
        and n_hours == 192
        and n_sites == 2 * LANES
        and n_sites * 2 == owners * 16
        and n_line * 16 == LANES
        and n_lines % 16 == 0
        and n_columns % LANES == 0
        and group_buses < EMPTY - LANES
        and window % (3 * LANES) == 0
        and last + window <= n_columns
    )
    if fits:
        return fast_device(*arrays)
    return general_device(*arrays)


def solution(mesh):
    in_specs = (
        P(None, ("line", "bus")),
        P(None, ("line", "bus")),
        P(None, ("line", "bus")),
        P(None, ("line", "bus")),
        P(None, ("line", "bus")),
        P(),
        P(),
        P(("line", "bus")),
        P(("line", "bus")),
        P(),
        P(),
        P(("line", "bus")),
        P(("line", "bus")),
        P("line", "bus"),
    )
    out_specs = P("line", "bus")
    return jax.shard_map(
        per_device, mesh=mesh, in_specs=in_specs, out_specs=out_specs, check_vma=False
    )
```

```python
import functools
import math

import jax
import jax.numpy as jnp
from jax import lax
from jax.experimental import pallas as pl
from jax.experimental.pallas import tpu as pltpu
from jax.sharding import PartitionSpec as P

BUSES = 70144
TILTS = 8
AZIMS = 12


solar_constant = 1367.0
albedo = 0.2
cos_limit = 0.08716
row_width = 36


def pick_table(classes, table, count):
    picked = jnp.zeros(classes.shape, jnp.float32)
    for entry in range(count):
        picked = jnp.where(classes == entry, table[entry], picked)
    return picked


def dirint_lookup(cell, dirint_coef):
    row_count = dirint_coef.shape[0] // row_width
    table = dirint_coef.reshape(row_count, row_width)
    flat_cell = cell.reshape(-1)
    upper = flat_cell // row_width
    lower = flat_cell % row_width
    row_pick = (upper[:, None] == jnp.arange(row_count, dtype=jnp.int32)[None, :]).astype(
        jnp.float32
    )
    rows = jnp.dot(
        row_pick, table, precision=lax.Precision.HIGHEST, preferred_element_type=jnp.float32
    )
    column_hit = lower[:, None] == jnp.arange(row_width, dtype=jnp.int32)[None, :]
    picked = jnp.sum(jnp.where(column_hit, rows, 0.0), axis=1)
    return picked.reshape(cell.shape)


def site_power(
    clear,
    cosz,
    sun_az,
    cell,
    sky,
    tilt_angle,
    array_azimuth,
    site_capacity,
    dirint_coef,
    perez_coef,
):
    global_flat = clear * solar_constant * cosz
    zenith = jnp.arccos(cosz)
    airmass = 1.0 / (cosz + 0.50572 * (96.07995 - zenith * (180.0 / math.pi)) ** (-1.6364))
    clear_beam = (
        0.866 - 0.122 * airmass + 0.0121 * airmass**2 - 0.000653 * airmass**3 + 1.4e-05 * airmass**4
    )
    part_a = 0.512 - 1.56 * clear + 2.286 * clear**2 - 2.222 * clear**3
    part_b = 0.37 + 0.962 * clear
    part_c = -0.28 + 0.932 * clear - 2.048 * clear**2
    beam_index = jnp.maximum(clear_beam - (part_a + part_b * jnp.exp(part_c * airmass)), 0.0)
    direct_normal = solar_constant * beam_index * dirint_lookup(cell, dirint_coef)
    diffuse = jnp.maximum(global_flat - direct_normal * cosz, 0.1 * global_flat)
    brightness = diffuse * airmass / solar_constant
    factors = [jnp.zeros(cosz.shape, jnp.float32) for entry in range(6)]
    for bin_index in range(perez_coef.shape[1]):
        hit = sky == bin_index
        factors = [jnp.where(hit, perez_coef[row, bin_index], factors[row]) for row in range(6)]
    circumsolar = jnp.maximum(0.0, factors[0] + factors[1] * brightness + factors[2] * zenith)
    horizon_term = factors[3] + factors[4] * brightness + factors[5] * zenith
    cos_tilt = jnp.cos(tilt_angle)
    sin_tilt = jnp.sin(tilt_angle)
    cos_incidence = cosz * cos_tilt + jnp.sin(zenith) * sin_tilt * jnp.cos(sun_az - array_azimuth)
    facing = jnp.maximum(cos_incidence, 0.0)
    horizon_cos = jnp.maximum(cosz, cos_limit)
    sky_part = diffuse * (
        (1.0 - circumsolar) * (1.0 + cos_tilt) * 0.5
        + circumsolar * facing / horizon_cos
        + horizon_term * sin_tilt
    )
    plane = direct_normal * facing + sky_part + albedo * global_flat * (1.0 - cos_tilt) * 0.5
    return (site_capacity * plane / 1000.0).astype(jnp.bfloat16)


def general_device(
    clearness,
    cos_zenith,
    sun_azimuth,
    dirint_cell,
    sky_bin,
    dirint_coef,
    perez_coef,
    tilt_class,
    azimuth_class,
    tilt_table,
    azimuth_table,
    capacity,
    site_bus,
    transfer_factors,
):
    line_count = lax.axis_size("line")
    bus_count = lax.axis_size("bus")
    owners = line_count * bus_count
    n_hours, n_sites = clearness.shape
    group_buses = BUSES // owners
    slots_each = max(2, 2 * n_sites // owners)
    tilt_angle = pick_table(tilt_class, tilt_table, TILTS)
    array_azimuth = pick_table(azimuth_class, azimuth_table, AZIMS)
    power = site_power(
        clearness,
        cos_zenith,
        sun_azimuth,
        dirint_cell,
        sky_bin,
        tilt_angle,
        array_azimuth,
        capacity,
        dirint_coef,
        perez_coef,
    )
    group_index = site_bus // group_buses
    target = group_index % line_count * bus_count + group_index // line_count
    local_bus = site_bus % group_buses
    one_hot = (target[:, None] == jnp.arange(owners, dtype=jnp.int32)[None, :]).astype(jnp.int32)
    position = jnp.sum(one_hot * (jnp.cumsum(one_hot, axis=0) - 1), axis=1)
    slot_index = target * slots_each + position
    outgoing = jnp.zeros((n_hours, owners * slots_each), jnp.bfloat16).at[:, slot_index].set(power)
    labels = jnp.zeros((1, owners * slots_each), jnp.int32).at[0, slot_index].set(local_bus)
    arrived, bus_tags = (
        lax.all_to_all(outgoing, ("line", "bus"), split_axis=1, concat_axis=1, tiled=True),
        lax.all_to_all(labels, ("line", "bus"), split_axis=1, concat_axis=1, tiled=True),
    )
    bus_tags = bus_tags.reshape(owners * slots_each)
    member = (bus_tags[:, None] == jnp.arange(group_buses, dtype=jnp.int32)[None, :]).astype(
        jnp.bfloat16
    )
    injection = jnp.einsum("hr,rb->bh", arrived, member, preferred_element_type=jnp.float32).astype(
        jnp.bfloat16
    )
    partial_flows = jnp.dot(
        transfer_factors,
        lax.all_gather(injection, "line", axis=0, tiled=True),
        preferred_element_type=jnp.float32,
    )
    return lax.psum_scatter(partial_flows, "bus", scatter_dimension=1, tiled=True)


LANES = 128
ACOS_POLY = (
    1.5707963262615365,
    -0.21460172591625612,
    0.08904479608150453,
    -0.0507408012983321,
    0.033314914408815,
    -0.02284457168134235,
    0.014575916928409219,
    -0.00744564558483129,
    0.002518626106102872,
    -0.00040427332732297214,
)
COS_POLY = tuple((-1.0) ** k / math.factorial(2 * k) for k in range(8))
SIN_POLY = tuple((-1.0) ** k / math.factorial(2 * k + 1) for k in range(8))
EMPTY = 4095


def horner(x, poly):
    total = jnp.full_like(x, poly[-1])
    for coefficient in poly[-2::-1]:
        total = total * x + coefficient
    return total


def reduce_pi(x):
    turns = jnp.floor(x * (1.0 / math.pi) + 0.5)
    rest = (x - turns * 3.140625) - turns * 0.0009676535897932
    odd = turns - 2.0 * jnp.floor(turns * 0.5)
    return rest, 1.0 - 2.0 * odd


def cosine(x):
    rest, sign = reduce_pi(x)
    return sign * horner(rest * rest, COS_POLY)


def sine(x):
    rest, sign = reduce_pi(x)
    return sign * rest * horner(rest * rest, SIN_POLY)


def to_column(row, eye):
    return jnp.sum(jnp.where(eye, row, 0.0), axis=1, keepdims=True)


def place_kernel(bus_ref, slot_ref, tags_ref, *, owners, group_buses, cap, n_line, n_bus):
    n_sites = bus_ref.shape[1]
    bus = bus_ref[...]
    group = jnp.zeros(bus.shape, jnp.int32)
    for k in range(1, owners):
        group = group + (bus >= k * group_buses).astype(jnp.int32)
    local = (bus - group * group_buses).astype(jnp.float32)
    group = group.astype(jnp.float32)
    first = lax.broadcasted_iota(jnp.int32, (n_sites, n_sites), 0)
    second = lax.broadcasted_iota(jnp.int32, (n_sites, n_sites), 1)
    eye = first == second
    earlier = (to_column(group, eye) == group) & (first < second)
    position = jnp.sum(jnp.where(earlier, 1.0, 0.0), axis=0, keepdims=True)
    slot = group * float(cap) + position
    slot_ref[...] = slot.astype(jnp.int32)
    slot_column = to_column(slot, eye).astype(jnp.int32)
    local_column = to_column(local, eye)
    n_slots = n_line * cap
    for bus_index in range(n_bus):
        lanes = lax.broadcasted_iota(jnp.int32, (n_sites, n_slots), 1) + bus_index * n_slots
        hit = slot_column == lanes
        tag = jnp.sum(jnp.where(hit, local_column + 1.0, 0.0), axis=0, keepdims=True)
        tag = jnp.where(tag > 0.5, tag - 1.0, float(EMPTY)).astype(jnp.int32)
        for line_index in range(n_line):
            row = line_index * n_bus + bus_index
            tags_ref[row : row + 1, :] = tag


def place_sites(site_bus, owners, group_buses, cap, n_line, n_bus):
    n_sites = site_bus.shape[0]
    return pl.pallas_call(
        functools.partial(
            place_kernel,
            owners=owners,
            group_buses=group_buses,
            cap=cap,
            n_line=n_line,
            n_bus=n_bus,
        ),
        out_shape=(
            jax.ShapeDtypeStruct((1, n_sites), jnp.int32),
            jax.ShapeDtypeStruct((owners, n_line * cap), jnp.int32),
        ),
        cost_estimate=pl.CostEstimate(flops=10**6, bytes_accessed=10**5, transcendentals=0),
        name="place",
    )(site_bus.reshape(1, n_sites))


def power_kernel(
    tilt_table_ref,
    azimuth_table_ref,
    perez_ref,
    *refs,
    n_line,
    n_bus,
    cap,
    rows,
):
    sources = refs[:10]
    out_ref = refs[10]
    held = refs[11:21]
    power_ref, dirint_rows, sems = refs[21:]
    copies = [
        pltpu.make_async_copy(source, place, sems.at[i])
        for i, (source, place) in enumerate(zip(sources, held))
    ]
    for copy in copies:
        copy.start()
    for copy in copies:
        copy.wait()
    clear_all, cosz_all, sun_all, cell_all, sky_all = held[:5]
    dirint_ref, tilt_class_ref, azimuth_class_ref, capacity_ref, slot_ref = held[5:]
    n_hours, n_sites = clear_all.shape
    cells = dirint_ref.shape[0]
    dirint_rows[...] = jnp.zeros_like(dirint_rows)
    for begin in range(0, cells, LANES):
        count = min(LANES, cells - begin)
        dirint_rows[:, begin : begin + count] = dirint_ref[begin : begin + count].reshape(1, count)
    tilt_class = tilt_class_ref[...]
    azimuth_class = azimuth_class_ref[...]
    tilt = jnp.zeros(tilt_class.shape, jnp.float32)
    for entry in range(TILTS):
        tilt = jnp.where(tilt_class == entry, tilt_table_ref[entry], tilt)
    azimuth = jnp.zeros(tilt_class.shape, jnp.float32)
    for entry in range(AZIMS):
        azimuth = jnp.where(azimuth_class == entry, azimuth_table_ref[entry], azimuth)
    wide = (rows, LANES)
    cos_tilts = cosine(tilt)
    sin_tilts = sine(tilt)
    capacity = capacity_ref[...]

    def some_hours(now, carry):
        at = pl.ds(pl.multiple_of(now * rows, rows), rows)
        for part in range(n_sites // LANES):
            lanes = slice(part * LANES, (part + 1) * LANES)
            cos_tilt = jnp.broadcast_to(cos_tilts[:, lanes], wide)
            sin_tilt = jnp.broadcast_to(sin_tilts[:, lanes], wide)
            array_azimuth = jnp.broadcast_to(azimuth[:, lanes], wide)
            site_capacity = jnp.broadcast_to(capacity[:, lanes], wide)
            clear = clear_all[at, lanes]
            cosz = cosz_all[at, lanes]
            sun_az = sun_all[at, lanes]
            cell = cell_all[at, lanes]
            sky = sky_all[at, lanes]
            global_flat = clear * solar_constant * cosz
            zenith = jnp.sqrt(1.0 - cosz) * horner(cosz, ACOS_POLY)
            sin_zenith = jnp.sqrt((1.0 - cosz) * (1.0 + cosz))
            height = 96.07995 - zenith * (180.0 / math.pi)
            airmass = 1.0 / (cosz + 0.50572 * jnp.exp(-1.6364 * jnp.log(height)))
            clear_beam = horner(airmass, (0.866, -0.122, 0.0121, -0.000653, 1.4e-05))
            part_a = horner(clear, (0.512, -1.56, 2.286, -2.222))
            part_b = 0.37 + 0.962 * clear
            part_c = horner(clear, (-0.28, 0.932, -2.048))
            beam = jnp.maximum(clear_beam - (part_a + part_b * jnp.exp(part_c * airmass)), 0.0)
            low = cell & (LANES - 1)
            high = cell >> 7
            coefficient = jnp.zeros(wide, jnp.float32)
            for row in range(dirint_rows.shape[1] // LANES):
                line = dirint_rows[:, row * LANES : (row + 1) * LANES]
                found = jnp.take_along_axis(
                    jnp.broadcast_to(line, wide), low, axis=1, mode="promise_in_bounds"
                )
                coefficient = jnp.where(high == row, found, coefficient)
            direct = solar_constant * beam * coefficient
            diffuse = jnp.maximum(global_flat - direct * cosz, 0.1 * global_flat)
            bright = diffuse * airmass * (1.0 / solar_constant)
            factor = [jnp.full(wide, perez_ref[row, 0]) for row in range(6)]
            for entry in range(1, perez_ref.shape[1]):
                hit = sky == entry
                factor = [
                    jnp.where(hit, perez_ref[row, entry], factor[row]) for row in range(6)
                ]
            circumsolar = jnp.maximum(0.0, factor[0] + factor[1] * bright + factor[2] * zenith)
            horizon = factor[3] + factor[4] * bright + factor[5] * zenith
            facing = jnp.maximum(
                cosz * cos_tilt + sin_zenith * sin_tilt * cosine(sun_az - array_azimuth), 0.0
            )
            sky_part = diffuse * (
                (1.0 - circumsolar) * (1.0 + cos_tilt) * 0.5
                + circumsolar * facing / jnp.maximum(cosz, cos_limit)
                + horizon * sin_tilt
            )
            plane = direct * facing + sky_part + albedo * global_flat * (1.0 - cos_tilt) * 0.5
            power_ref[at, lanes] = (site_capacity * plane / 1000.0).astype(jnp.bfloat16)
        return carry

    lax.fori_loop(0, n_hours // rows, some_hours, 0)
    power = power_ref[...]
    low_hours = power[:LANES]
    rest = power[LANES:]
    blank = jnp.zeros_like(rest)
    left = jnp.concatenate([rest, blank], axis=0)
    right = jnp.concatenate([blank, rest], axis=0)
    slot = slot_ref[...]
    n_slots = n_line * cap
    half = cap // 2
    dims = (((1,), (1,)), ((), ()))
    for bus_index in range(n_bus):
        base = bus_index * n_slots
        slots = lax.broadcasted_iota(jnp.int32, (n_slots, n_sites), 0) + base
        pick = jnp.where(slots == slot, 1.0, 0.0).astype(jnp.bfloat16)
        top = lax.dot_general(pick, low_hours, dims, preferred_element_type=jnp.float32)
        index = lax.broadcasted_iota(jnp.int32, (n_slots // 2, n_sites), 0)
        paired = (index // half) * cap + index % half + base
        pick_left = jnp.where(paired == slot, 1.0, 0.0).astype(jnp.bfloat16)
        pick_right = jnp.where(paired + half == slot, 1.0, 0.0).astype(jnp.bfloat16)
        bottom = lax.dot_general(
            pick_left, left, dims, preferred_element_type=jnp.float32
        ) + lax.dot_general(pick_right, right, dims, preferred_element_type=jnp.float32)
        top = top.astype(jnp.bfloat16)
        bottom = bottom.astype(jnp.bfloat16)
        for line_index in range(n_line):
            row = line_index * n_bus + bus_index
            out_ref[row, :n_slots, :] = top
            out_ref[row, n_slots:, :] = bottom


def packed_power(
    tilt_table,
    azimuth_table,
    hourly,
    dirint_coef,
    perez_coef,
    tilt_class,
    azimuth_class,
    capacity,
    slot,
    n_line,
    n_bus,
    cap,
):
    n_hours, n_sites = hourly[0].shape
    owners = n_line * n_bus
    n_slots = n_line * cap
    cells = dirint_coef.shape[0]
    rows = 64
    smem = pl.BlockSpec(memory_space=pltpu.SMEM)
    shape = (owners, n_slots * n_hours // LANES, LANES)
    operands = (
        *hourly,
        dirint_coef,
        tilt_class.reshape(1, n_sites),
        azimuth_class.reshape(1, n_sites),
        capacity.reshape(1, n_sites),
        slot,
    )
    return pl.pallas_call(
        functools.partial(power_kernel, n_line=n_line, n_bus=n_bus, cap=cap, rows=rows),
        out_shape=jax.ShapeDtypeStruct(shape, jnp.bfloat16),
        in_specs=[smem] * 3 + [pl.BlockSpec(memory_space=pltpu.HBM)] * len(operands),
        out_specs=pl.BlockSpec(memory_space=pltpu.VMEM),
        scratch_shapes=[pltpu.VMEM(x.shape, x.dtype) for x in operands]
        + [
            pltpu.VMEM((n_hours, n_sites), jnp.bfloat16),
            pltpu.VMEM((1, -(-cells // LANES) * LANES), jnp.float32),
            pltpu.SemaphoreType.DMA((len(operands),)),
        ],
        compiler_params=pltpu.CompilerParams(vmem_limit_bytes=64 << 20),
        cost_estimate=pl.CostEstimate(
            flops=2 * 10**8, bytes_accessed=3 * 10**6, transcendentals=2 * 10**5
        ),
        name="power",
    )(tilt_table, azimuth_table, perez_coef, *operands)


def order_slots(tags_ref, sorted_ref, rank_ref, plan_ref, group_buses):
    n_groups, n_slots = tags_ref.shape
    half = n_slots // 2
    tags = tags_ref[...].astype(jnp.float32)
    lanes = lax.broadcasted_iota(jnp.int32, (n_slots, n_slots), 1).astype(jnp.float32)
    index = lax.broadcasted_iota(jnp.int32, (n_groups, n_slots), 1)
    keys = tags * n_slots + index.astype(jnp.float32)
    tag_columns = jnp.transpose(tags)
    key_columns = jnp.transpose(keys)
    ranks = []
    for g in range(n_groups):
        smaller = key_columns[:, g : g + 1] < keys[g : g + 1]
        ranks.append(jnp.sum(jnp.where(smaller, 1.0, 0.0), axis=0, keepdims=True))
    rank = jnp.concatenate(ranks, axis=0)
    rank_ref[...] = rank.astype(jnp.int32)
    rank_columns = jnp.transpose(rank)
    ordered = []
    for g in range(n_groups):
        hit = rank_columns[:, g : g + 1] == lanes
        found = jnp.sum(jnp.where(hit, tag_columns[:, g : g + 1], 0.0), axis=0, keepdims=True)
        ordered.append(found + float(g * group_buses % LANES))
    ordered = jnp.concatenate(ordered, axis=0)
    sorted_ref[...] = ordered.astype(jnp.int32)
    real = ordered < float(EMPTY)
    last = jnp.max(jnp.where(real & (index < half), ordered, 0.0), axis=1, keepdims=True)
    after = jnp.min(jnp.where(real & (index >= half), ordered, 2.0 * EMPTY), axis=1, keepdims=True)
    for g in range(n_groups):
        plan_ref[0, g] = jnp.max(last[g : g + 1]).astype(jnp.int32)
        plan_ref[1, g] = jnp.max(after[g : g + 1]).astype(jnp.int32)


def select_kernel(
    tags_ref,
    factors_ref,
    out_ref,
    rank_ref,
    buffer,
    pick,
    sorted_ref,
    plan_ref,
    sems,
    *,
    group_buses,
    window,
    seg,
):
    g = pl.program_id(0)
    n_groups = pl.num_programs(0)
    n_slots = out_ref.shape[1]
    half = n_slots // 2
    n_seg = window // seg

    def copy(index):
        start = pl.multiple_of((index * group_buses) // LANES * LANES, LANES)
        slot = lax.rem(index, 2)
        return pltpu.make_async_copy(
            factors_ref.at[:, pl.ds(start, window)], buffer.at[slot], sems.at[slot]
        )

    @pl.when(g == 0)
    def _():
        copy(g).start()

    @pl.when(g + 1 < n_groups)
    def _():
        copy(g + 1).start()

    @pl.when(g == 0)
    def _():
        order_slots(tags_ref, sorted_ref, rank_ref, plan_ref, group_buses)

    last = plan_ref[0, g]
    after = plan_ref[1, g]
    place = sorted_ref[pl.ds(g, 1), :]

    def wanted(chunk, k):
        if chunk == 0:
            return last >= k * seg
        return after < (k + 1) * seg

    for chunk in range(2):
        columns = slice(chunk * half, (chunk + 1) * half)
        for k in range(n_seg):

            @pl.when(wanted(chunk, k))
            def _():
                buses = lax.broadcasted_iota(jnp.int32, (seg, half), 0) + k * seg
                pick[k * seg : (k + 1) * seg, columns] = jnp.where(
                    buses == place[:, columns], 1.0, 0.0
                ).astype(jnp.bfloat16)

    copy(g).wait()
    now = lax.rem(g, 2)
    for k in range(n_seg):
        stop = (k + 1) * seg
        begin = k * seg
        ends_here = last < stop if k + 1 < n_seg else last >= begin
        if 0 < k < n_seg - 1:
            ends_here = ends_here & (last >= begin)

        @pl.when(ends_here)
        def _():
            out_ref[:, :half] = jnp.dot(
                buffer[now, :, :stop], pick[:stop, :half], preferred_element_type=jnp.float32
            ).astype(jnp.bfloat16)

        starts_here = after < stop
        if k:
            starts_here = starts_here & (after >= begin)

        @pl.when(starts_here)
        def _():
            out_ref[:, half:] = jnp.dot(
                buffer[now, :, begin:], pick[begin:, half:], preferred_element_type=jnp.float32
            ).astype(jnp.bfloat16)

    @pl.when(after >= window)
    def _():
        out_ref[:, half:] = jnp.zeros((out_ref.shape[0], half), jnp.bfloat16)


def select_columns(tags, factors, group_buses, window, seg):
    n_groups, n_slots = tags.shape
    n_lines = factors.shape[0]
    whole = pl.BlockSpec((n_groups, n_slots), lambda g: (0, 0))
    return pl.pallas_call(
        functools.partial(select_kernel, group_buses=group_buses, window=window, seg=seg),
        grid=(n_groups,),
        in_specs=[whole, pl.BlockSpec(memory_space=pltpu.HBM)],
        out_specs=(pl.BlockSpec((n_lines, n_slots), lambda g: (0, g)), whole),
        out_shape=(
            jax.ShapeDtypeStruct((n_lines, n_groups * n_slots), jnp.bfloat16),
            jax.ShapeDtypeStruct((n_groups, n_slots), jnp.int32),
        ),
        scratch_shapes=[
            pltpu.VMEM((2, n_lines, window), jnp.bfloat16),
            pltpu.VMEM((window, n_slots), jnp.bfloat16),
            pltpu.VMEM((n_groups, n_slots), jnp.int32),
            pltpu.SMEM((2, n_groups), jnp.int32),
            pltpu.SemaphoreType.DMA((2,)),
        ],
        compiler_params=pltpu.CompilerParams(vmem_limit_bytes=48 << 20),
        cost_estimate=pl.CostEstimate(
            flops=2 * n_lines * window * n_groups * n_slots,
            bytes_accessed=2 * n_lines * window * n_groups,
            transcendentals=0,
        ),
        name="select",
    )(tags, factors)


def move_power(rank_ref, arrived_ref, moved_ref, cap):
    n_groups, n_slots = rank_ref.shape
    half = cap // 2
    tops = n_groups * cap
    places = lax.broadcasted_iota(jnp.int32, (n_slots, n_slots), 0)

    def one(g, carry):
        top_at = pl.ds(pl.multiple_of(g * cap, cap), cap)
        bottom_at = pl.ds(pl.multiple_of(tops + g * half, half), half)
        top = arrived_ref[:, top_at, :].reshape(n_slots, LANES)
        bottom = arrived_ref[:, bottom_at, :].astype(jnp.float32)
        blocks = bottom.shape[0]
        turned = pltpu.roll(bottom.reshape(blocks * half, LANES), LANES // 2, 1)
        bottom = jnp.concatenate([bottom, turned.reshape(blocks, half, LANES)], axis=1)
        bottom = bottom.reshape(n_slots, LANES).astype(jnp.bfloat16)
        power = jnp.concatenate([top, bottom], axis=1)
        move = jnp.where(places == rank_ref[pl.ds(g, 1), :], 1.0, 0.0).astype(jnp.bfloat16)
        moved = jnp.dot(move, power, preferred_element_type=jnp.float32)
        moved_ref[pl.ds(pl.multiple_of(g * n_slots, n_slots), n_slots), :] = moved.astype(
            jnp.bfloat16
        )
        return carry

    lax.fori_loop(0, n_groups, one, 0, unroll=2)


def lines_kernel(
    core_ref, *refs, cap, begin, count, first
):
    if first:
        rank_ref, arrived_ref, picked_ref = refs[:3]
        keep_ref, send_ref, moved_out, moved_ref, buffer, sems = refs[3:]
    else:
        moved_in, picked_ref = refs[:2]
        keep_ref, send_ref, moved_ref, buffer, sems = refs[2:]
    n_blocks = sems.shape[0] - 1
    block = keep_ref.shape[2] // n_blocks
    last_size = count - (n_blocks - 1) * block

    def copy(i, size):
        at = pl.multiple_of(i * block, 16)
        return pltpu.make_async_copy(
            picked_ref.at[pl.ds(begin + at, size)], buffer.at[pl.ds(at, size)], sems.at[i]
        )

    def each(act):
        for i in range(n_blocks):
            act(copy(i, block if i + 1 < n_blocks else last_size))

    if first:
        each(lambda c: c.start())
        move_power(rank_ref, arrived_ref, moved_ref, cap)
        out = pltpu.make_async_copy(moved_ref, moved_out, sems.at[n_blocks])
        out.start()
    else:
        fetch = pltpu.make_async_copy(moved_in, moved_ref, sems.at[n_blocks])
        fetch.start()
        each(lambda c: c.start())
        fetch.wait()
    rows_each = keep_ref.shape[1]
    core_zero = core_ref[0] == 0

    def one(i, carry):
        @pl.when(i + 1 < n_blocks)
        def _():
            copy(i, block).wait()

        @pl.when(i + 1 == n_blocks)
        def _():
            copy(i, last_size).wait()

        at = pl.multiple_of(i * block, block)
        flow = jnp.dot(
            buffer[pl.ds(at, block), :], moved_ref[...], preferred_element_type=jnp.float32
        )
        turned = jnp.transpose(flow)
        for x in range(keep_ref.shape[0]):
            low = 2 * x * rows_each
            even = turned[low : low + rows_each]
            odd = turned[low + rows_each : low + 2 * rows_each]
            keep_ref[x, :, pl.ds(at, block)] = jnp.where(core_zero, even, odd)
            away = jnp.where(core_zero, odd, even)
            send_ref[x, :, pl.ds(at, block)] = away.astype(jnp.bfloat16)
        return carry

    lax.fori_loop(0, n_blocks, one, 0)
    if first:
        out.wait()


def lines(core, inputs, picked, shape, cap, begin, count, padded, moved_shape, first):
    smem = pl.BlockSpec(memory_space=pltpu.SMEM)
    vmem = pl.BlockSpec(memory_space=pltpu.VMEM)
    hbm = pl.BlockSpec(memory_space=pltpu.HBM)
    part = jax.ShapeDtypeStruct(shape + (padded,), jnp.float32)
    sent = jax.ShapeDtypeStruct(shape + (padded,), jnp.bfloat16)
    moved = jax.ShapeDtypeStruct(moved_shape, jnp.bfloat16)
    block = 512
    return pl.pallas_call(
        functools.partial(lines_kernel, cap=cap, begin=begin, count=count, first=first),
        in_specs=[smem] + ([vmem, vmem] if first else [hbm]) + [hbm],
        out_specs=[vmem, vmem] + ([hbm] if first else []),
        out_shape=[part, sent] + ([moved] if first else []),
        scratch_shapes=[
            pltpu.VMEM(moved_shape, jnp.bfloat16),
            pltpu.VMEM((padded, picked.shape[1]), jnp.bfloat16),
            pltpu.SemaphoreType.DMA((padded // block + 1,)),
        ],
        compiler_params=pltpu.CompilerParams(vmem_limit_bytes=46 << 20),
        cost_estimate=pl.CostEstimate(
            flops=1 * 2 * count * moved_shape[0] * moved_shape[1],
            bytes_accessed=1 * 2 * count * moved_shape[0],
            transcendentals=0,
        ),
        name="first_lines" if first else "other_lines",
    )(core, *inputs, picked)


def fast_device(
    clearness,
    cos_zenith,
    sun_azimuth,
    dirint_cell,
    sky_bin,
    dirint_coef,
    perez_coef,
    tilt_class,
    azimuth_class,
    tilt_table,
    azimuth_table,
    capacity,
    site_bus,
    transfer_factors,
):
    n_line = lax.axis_size("line")
    n_bus = lax.axis_size("bus")
    owners = n_line * n_bus
    n_hours, n_sites = clearness.shape
    n_lines, n_columns = transfer_factors.shape
    group_buses = BUSES // owners
    cap = 2 * n_sites // owners
    window = window_of(group_buses)
    seg = window // 3
    slot, tags = place_sites(site_bus, owners, group_buses, cap, n_line, n_bus)
    tags = lax.all_to_all(tags, ("line", "bus"), split_axis=0, concat_axis=0, tiled=True)
    outgoing = packed_power(
        tilt_table,
        azimuth_table,
        (clearness, cos_zenith, sun_azimuth, dirint_cell, sky_bin),
        dirint_coef,
        perez_coef,
        tilt_class,
        azimuth_class,
        capacity,
        slot,
        n_line,
        n_bus,
        cap,
    )
    arrived = lax.all_to_all(outgoing, ("line", "bus"), split_axis=0, concat_axis=0, tiled=True)
    tags = tags.reshape(owners, n_line, cap).transpose(1, 0, 2).reshape(n_line, owners * cap)
    picked, rank = select_columns(tags, transfer_factors, group_buses, window, seg)
    place = lax.axis_index("bus")
    core = (place % 2).reshape(1)
    near = place // 2 == 0
    other_core = [(i, i ^ 1) for i in range(n_bus)]
    other_chip = [(i, i ^ 2) for i in range(n_bus)]
    shape = (n_bus // 2, n_hours // n_bus)
    moved_shape = (n_line * owners * cap, 2 * LANES)
    half_lines = -(-n_lines // 1024) * 512
    keep_a, send_a, moved = lines(
        core, (rank, arrived), picked, shape, cap, 0, half_lines, half_lines, moved_shape, True
    )
    other = n_lines - half_lines
    padded = -(-other // 512) * 512
    keep_b, send_b = lines(
        core, (moved,), picked, shape, cap, half_lines, other, padded, moved_shape, False
    )
    ends = []
    for keep, send in ((keep_a, send_a), (keep_b, send_b)):
        summed = keep + lax.ppermute(send, "bus", other_core).astype(jnp.float32)
        own = jnp.where(near, summed[0], summed[1])
        away = jnp.where(near, summed[1], summed[0]).astype(jnp.bfloat16)
        away = lax.ppermute(away, "bus", other_chip)
        ends.append(own + away.astype(jnp.float32))
    return jnp.concatenate(ends, axis=1)[:, :n_lines].T


def window_of(group_buses):
    step = math.gcd(group_buses, LANES)
    most = LANES - step + group_buses
    return -(-most // LANES) * LANES


def per_device(*arrays):
    n_line = lax.axis_size("line")
    n_bus = lax.axis_size("bus")
    owners = n_line * n_bus
    n_hours, n_sites = arrays[0].shape
    n_lines, n_columns = arrays[-1].shape
    group_buses = BUSES // owners
    window = window_of(group_buses)
    last = (n_line - 1) * group_buses // LANES * LANES
    fits = (
        n_bus == 4
        and n_hours == 192
        and n_sites == 2 * LANES
        and n_sites * 2 == owners * 16
        and n_line * 16 == LANES
        and n_lines % 16 == 0
        and n_columns % LANES == 0
        and group_buses < EMPTY - LANES
        and window % (3 * LANES) == 0
        and last + window <= n_columns
    )
    if fits:
        return fast_device(*arrays)
    return general_device(*arrays)


def solution(mesh):
    in_specs = (
        P(None, ("line", "bus")),
        P(None, ("line", "bus")),
        P(None, ("line", "bus")),
        P(None, ("line", "bus")),
        P(None, ("line", "bus")),
        P(),
        P(),
        P(("line", "bus")),
        P(("line", "bus")),
        P(),
        P(),
        P(("line", "bus")),
        P(("line", "bus")),
        P("line", "bus"),
    )
    out_specs = P("line", "bus")
    return jax.shard_map(
        per_device, mesh=mesh, in_specs=in_specs, out_specs=out_specs, check_vma=False
    )
```
